32 devices in a mesh: seq: 16 (over z, y, core), chan: 2 (over x).
Axes of the slice: x: 2, y: 2, z: 4, core: 2. Of those that a mesh axis runs over, the one named last changes fastest.
Arguments:
- stream_in: bfloat16 [4096, 4096], P('seq'), may hold values from -6 to 6
- mr_proj: bfloat16 [4096, 3, 4096], P('seq', None, 'chan'), may hold values from -6 to 6
- mr_short: float32 [3, 3, 4096], P(None, None, 'chan'), may hold values from -3 to 3
- mr_filter: float32 [256, 128], P('chan'), may hold values from -0.5 to 0.5
- mr_out: bfloat16 [4096, 4096], P('chan', 'seq'), may hold values from -0.09375 to 0.09375
- li_gain: float32 [4096], replicated, may hold values from 0.5 to 1.5
- li_in: bfloat16 [4096, 3, 4096], P('seq', None, 'chan'), may hold values from -0.09375 to 0.09375
- li_short: float32 [3, 3, 4096], P(None, None, 'chan'), may hold values from -3 to 3
- li_res: float32 [16, 4096], P(None, 'chan'), may hold values from -0.09 to 0.09
- li_rate: float32 [16, 4096], P(None, 'chan'), may hold values from 0.00012207031 to 0.05
- li_skip: float32 [4096], P('chan'), may hold values from -4 to 4
Outputs:
- stream_out: bfloat16 [4096, 4096], P('seq', 'chan')
- li_output: bfloat16 [4096, 4096], P('chan', 'seq')
The draws below stay inside these ranges and needn't reach their ends.
All inputs are finite; a program needn't handle non-finite values.
Results may differ from the reference program's by a relative error of at most 0.04.
Values may be sent and summed in bfloat16 or wider, within the bound.
A program may use at most 128 MiB of HBM per device.

```python
import math
import jax
import jax.numpy as jnp
from jax import lax

D = 4096
KMR = 128
GROUP = 16
MODES = 16
SEQ_LEN = 4096
GROUPS = 256


def block_scale(own_key, dims, split, low, high):
    level, own = 1.0, jax.random.fold_in(own_key, 6)
    for axis_at, parts in split:
        draws = jnp.exp(jax.random.uniform(jax.random.fold_in(own, axis_at), (parts,), jnp.float32, low / len(split), high / len(split)))
        level = level * jnp.repeat(draws, dims[axis_at] // parts).reshape([-1 if axis == axis_at else 1 for axis in range(len(dims))])
    return level


def centred(key, shape, spread, limit, shards=(), kind=jnp.bfloat16):
    result = jax.random.normal(key, shape, jnp.float32) * spread
    if len(shards) > 0:
        result = block_scale(key, shape, shards, -0.22, 0.18) * result
    return jnp.clip(result, min=-limit, max=limit).astype(kind)


def setup_inputs(seed: int = 0) -> dict:
    key_list = jax.random.split(jax.random.key(seed), 12)
    stream_in = centred(key_list[0], (SEQ_LEN, D), 1.0, 6.0, ((0, 16),))
    mr_proj = centred(key_list[1], (SEQ_LEN, 3, D), 1.0, 6.0, ((0, 16), (2, 2)))
    mr_short = centred(key_list[2], (3, 3, D), 0.6, 3.0, ((2, 2),), jnp.float32)
    mr_filter = centred(key_list[3], (GROUPS, KMR), KMR ** -0.5, 0.5, ((0, 2),), jnp.float32)
    mr_out = centred(key_list[4], (D, D), D ** -0.5, 0.09375, ((0, 2), (1, 16)))
    li_gain = jnp.clip(1.0 + 0.1 * jax.random.normal(key_list[5], (D,), jnp.float32), 0.5, 1.5)
    li_in = centred(key_list[6], (D, 3, D), D ** -0.5, 0.09375, ((0, 16), (2, 2)))
    li_short = centred(key_list[7], (3, 3, D), 0.6, 3.0, ((2, 2),), jnp.float32)
    li_res = centred(key_list[8], (MODES, D), 0.015, 0.09, ((1, 2),), jnp.float32)
    li_rate = jnp.clip(jnp.exp(math.log(0.05) - 6.015181 * jax.random.uniform(key_list[9], (MODES, D), jnp.float32) ** block_scale(key_list[9], (MODES, D), ((1, 2),), -0.2, 0.2)), 0.00012207031, 0.05)
    li_skip = centred(key_list[10], (D,), 1.0, 4.0, ((0, 2),), jnp.float32)
    return dict(stream_in=stream_in, mr_proj=mr_proj, mr_short=mr_short, mr_filter=mr_filter, mr_out=mr_out, li_gain=li_gain, li_in=li_in, li_short=li_short, li_res=li_res, li_rate=li_rate, li_skip=li_skip)


EPSILON = 1e-06
HIGHEST = lax.Precision.HIGHEST

def short_filter(raw_rows, weights):
    row_count = raw_rows.shape[0]
    padded = jnp.concatenate([jnp.zeros((2,) + raw_rows.shape[1:], raw_rows.dtype), raw_rows], axis=0)
    running = weights[:, 0][None] * padded[2:2 + row_count]
    for lag_index in (1, 2):
        running = running + weights[:, lag_index][None] * padded[2 - lag_index:2 - lag_index + row_count]
    return running

def grouped_filter(values, filters):
    per_channel = jnp.repeat(filters, GROUP, axis=0)
    row_count = values.shape[0]
    tap_count = filters.shape[1]
    padded = jnp.concatenate([jnp.zeros((tap_count - 1, values.shape[1]), values.dtype), values], axis=0)

    def one_tap(lag_index, running):
        window = lax.dynamic_slice_in_dim(padded, tap_count - 1 - lag_index, row_count, 0)
        column = lax.dynamic_index_in_dim(per_channel, lag_index, 1, keepdims=False)
        return running + column[None] * window
    return lax.fori_loop(0, tap_count, one_tap, jnp.zeros_like(values))

def modal_long_filter(values, residues, rates, skip_gain):
    seq_length, chan_count = values.shape
    block_width = min(128, chan_count)
    block_count = chan_count // block_width
    lag_steps = jnp.arange(seq_length, dtype=jnp.float32)
    fft_length = 2 * seq_length

    def one_block(pieces_in):
        section, residue_set, rate_set, gain_set = pieces_in
        kernel = jnp.einsum('br,brl->bl', residue_set, jnp.exp(-rate_set[:, :, None] * lag_steps), precision=HIGHEST)
        spectrum = jnp.fft.rfft(section, n=fft_length) * jnp.fft.rfft(kernel, n=fft_length)
        convolved = jnp.fft.irfft(spectrum, n=fft_length)[:, :seq_length]
        return convolved + gain_set[:, None] * section
    channel_major = values.T.reshape(block_count, block_width, seq_length)
    residue_blocks = residues.T.reshape(block_count, block_width, residues.shape[0])
    rate_blocks = rates.T.reshape(block_count, block_width, rates.shape[0])
    gain_blocks = skip_gain.reshape(block_count, block_width)
    outputs = lax.map(one_block, (channel_major, residue_blocks, rate_blocks, gain_blocks))
    return outputs.reshape(chan_count, seq_length)

def reference(stream_in, mr_proj, mr_short, mr_filter, mr_out, li_gain, li_in, li_short, li_res, li_rate, li_skip):
    mr_mixed = short_filter(mr_proj.astype(jnp.float32), mr_short.astype(jnp.float32))
    mr_values = mr_mixed[:, 1] * mr_mixed[:, 2]
    mr_filtered = grouped_filter(mr_values, mr_filter.astype(jnp.float32))
    mr_gated = (mr_mixed[:, 0] * mr_filtered).astype(jnp.bfloat16)
    branch = jnp.dot(mr_gated, mr_out, preferred_element_type=jnp.float32)
    stream_out = (stream_in.astype(jnp.float32) + branch).astype(jnp.bfloat16)
    stream_wide = stream_out.astype(jnp.float32)
    inverse_rms = lax.rsqrt(lax.optimization_barrier(jnp.mean(stream_wide * stream_wide, axis=1, keepdims=True)) + EPSILON)
    normed = (stream_wide * inverse_rms * li_gain.astype(jnp.float32)[None]).astype(jnp.bfloat16)
    width_d = normed.shape[1]
    li_proj = jnp.dot(normed, li_in.reshape(width_d, 3 * width_d), preferred_element_type=jnp.float32)
    li_proj = li_proj.reshape(-1, 3, width_d).astype(jnp.bfloat16)
    li_mixed = short_filter(li_proj.astype(jnp.float32), li_short.astype(jnp.float32))
    li_values = (li_mixed[:, 1] * li_mixed[:, 2]).astype(jnp.bfloat16)
    li_filtered = modal_long_filter(li_values.astype(jnp.float32), li_res.astype(jnp.float32), li_rate.astype(jnp.float32), li_skip.astype(jnp.float32))
    li_output = (li_mixed[:, 0].T * li_filtered).astype(jnp.bfloat16)
    return (stream_out, li_output)
```

```python
import functools

import jax
import jax.numpy as jnp
from jax import lax
from jax.experimental import pallas as pl
from jax.experimental.pallas import tpu as pltpu
from jax.sharding import PartitionSpec as P

GROUP = 16


EPSILON = 1e-06
HIGHEST = lax.Precision.HIGHEST


def passed_along(block, axis, distance):
    devices = range(lax.axis_size(axis))
    route = [(i - distance, i) for i in devices if i - distance in devices]
    return lax.ppermute(block, axis, route)


def band_matrices(filters):
    tap_count = filters.shape[1]
    out_index = jnp.arange(tap_count, dtype=jnp.int32)[:, None, None]
    in_index = jnp.arange(2 * tap_count, dtype=jnp.int32)[None, :, None]
    lag_index = jnp.arange(tap_count, dtype=jnp.int32)[None, None, :]
    selector = (out_index + tap_count - 1 - in_index == lag_index).astype(jnp.bfloat16)
    return jnp.einsum(
        "gj,isj->gis", filters.astype(jnp.bfloat16), selector, preferred_element_type=jnp.float32
    ).astype(jnp.bfloat16)


def lagged_rows(extended, weights, row_count):
    running = weights[:, 0][None] * extended[2 : 2 + row_count]
    for lag_index in (1, 2):
        running = (
            running
            + weights[:, lag_index][None] * extended[2 - lag_index : 2 - lag_index + row_count]
        )
    return running


def swapped(blocks, axis):
    count = lax.axis_size(axis)
    if count != 2:
        return lax.all_to_all(blocks, axis, split_axis=0, concat_axis=0, tiled=True)
    me = lax.axis_index(axis)
    mine = lax.dynamic_index_in_dim(blocks, me, 0, keepdims=False)
    other = lax.dynamic_index_in_dim(blocks, 1 - me, 0, keepdims=False)
    received = lax.ppermute(other, axis, [(0, 1), (1, 0)])
    first = me == 0
    return jnp.stack([jnp.where(first, mine, received), jnp.where(first, received, mine)])


def scattered(blocks, axis):
    count = lax.axis_size(axis)
    me = lax.axis_index(axis)
    chips, chip = count // 2, me // 2
    pairs = blocks.reshape((chips, 2) + blocks.shape[1:])
    pieces = []
    for k in range(chips):
        piece = lax.dynamic_index_in_dim(pairs, lax.rem(chip + k, chips), 0, keepdims=False)
        if k:
            route = [(i, (i + 2 * k) % count) for i in range(count)]
            piece = lax.ppermute(piece, axis, route)
        pieces.append(piece)
    return pieces


def assembled(pieces, axis):
    count = lax.axis_size(axis)
    me = lax.axis_index(axis)
    chips, chip, core = count // 2, me // 2, lax.rem(me, 2)
    kept = jnp.stack([lax.dynamic_index_in_dim(p, core, 0, keepdims=False) for p in pieces])
    given = jnp.stack([lax.dynamic_index_in_dim(p, 1 - core, 0, keepdims=False) for p in pieces])
    taken = lax.ppermute(given, axis, [(i, i ^ 1) for i in range(count)])
    both = jnp.stack(
        [jnp.where(core == 0, kept, taken), jnp.where(core == 0, taken, kept)], axis=1
    )
    both = both[::-1]
    return lax.dynamic_slice_in_dim(
        jnp.concatenate([both, both]), lax.rem(2 * chips - 1 - chip, chips), chips, 0
    )


def branch_kernel(gated_ref, weights_ref, out_ref):
    out_ref[...] = jnp.dot(gated_ref[...], weights_ref[0], preferred_element_type=jnp.float32)


def branch_product(gated, weights):
    rows, depth = gated.shape
    blocks, _, columns = weights.shape
    return pl.pallas_call(
        branch_kernel,
        out_shape=jax.ShapeDtypeStruct((rows, blocks * columns), jnp.float32),
        grid=(blocks,),
        in_specs=[
            pl.BlockSpec((rows, depth), lambda i: (0, 0)),
            pl.BlockSpec((1, depth, columns), lambda i: (i, 0, 0)),
        ],
        out_specs=pl.BlockSpec((rows, columns), lambda i: (0, i)),
        cost_estimate=pl.CostEstimate(
            flops=2 * rows * depth * blocks * columns,
            bytes_accessed=2 * blocks * depth * columns,
            transcendentals=0,
        ),
    )(gated, weights)


PARTS = 4


def ring_kernel(chips, swaps, *refs):
    inputs, outputs, sems = refs[: 1 + swaps], refs[1 + swaps : 2 + 2 * swaps], refs[2 + 2 * swaps :]
    block_ref, out_ref = inputs[0], outputs[0]
    ring_send, ring_recv, core_send, core_recv, own_sem, swap_send, swap_recv = sems
    me = lax.axis_index("seq")
    core = lax.rem(me, 2)
    chip = me // 2
    row, column = chip // 2, lax.rem(chip, 2)
    place = row + column * (chips - 1 - 2 * row)
    sibling = me + 1 - 2 * core
    rows = block_ref.shape[0] // PARTS

    def device(position, core_index):
        position = lax.rem(position + 2 * chips, chips)
        second = position // (chips // 2)
        at_row = position + second * (chips - 1 - 2 * position)
        return (2 * at_row + second) * 2 + core_index

    following, preceding = device(place + 1, core), device(place - 1, core)
    barrier = pltpu.get_barrier_semaphore()
    for target in (following, preceding, sibling):
        pl.semaphore_signal(barrier, inc=1, device_id={"seq": target})
    if swaps:
        partner = 1 - lax.axis_index("chan")
        pl.semaphore_signal(barrier, inc=1, device_id={"chan": partner})
    pl.semaphore_wait(barrier, 4 if swaps else 3)

    def ring(way, step, half, source, slot):
        part = pl.ds((2 * way + half) * rows, rows)
        index = (way * (chips - 1) + step) * 2 + half
        return pltpu.make_async_remote_copy(
            src_ref=source.at[part],
            dst_ref=out_ref.at[slot, part],
            send_sem=ring_send.at[index],
            recv_sem=ring_recv.at[index],
            device_id={"seq": (following, preceding)[way]},
        )

    def across(way, step, half, source, slot):
        part = pl.ds((2 * way + half) * rows, rows)
        index = (way * chips + step) * 2 + half
        return pltpu.make_async_remote_copy(
            src_ref=source.at[part],
            dst_ref=out_ref.at[slot, part],
            send_sem=core_send.at[index],
            recv_sem=core_recv.at[index],
            device_id={"seq": sibling},
        )

    started = []
    for step in range(chips):
        for half in (0, 1):
            for way in (0, 1):
                slot = device(place + (2 * way - 1) * step, core)
                source = block_ref if step == 0 else out_ref.at[slot]
                if step:
                    ring(way, step - 1, half, source, slot).wait_recv()
                if step < chips - 1:
                    copy = ring(way, step, half, source, slot)
                    copy.start()
                    started.append(copy)
                copy = across(way, step, half, source, slot)
                copy.start()
                started.append(copy)
        if step == 0:
            for i in range(swaps):
                copy = pltpu.make_async_remote_copy(
                    src_ref=inputs[1 + i],
                    dst_ref=outputs[1 + i],
                    send_sem=swap_send.at[i],
                    recv_sem=swap_recv.at[i],
                    device_id={"chan": partner},
                )
                copy.start()
                started.append(copy)
            own = pltpu.make_async_copy(block_ref, out_ref.at[me], own_sem)
            own.start()
    for step in range(chips):
        for half in (0, 1):
            for way in (0, 1):
                slot = device(place + (2 * way - 1) * step, 1 - core)
                across(way, step, half, out_ref.at[slot], slot).wait_recv()
    own.wait()
    for copy in started:
        copy.wait_send()
    for i in range(swaps):
        pltpu.make_async_remote_copy(
            src_ref=inputs[1 + i],
            dst_ref=outputs[1 + i],
            send_sem=swap_send.at[i],
            recv_sem=swap_recv.at[i],
            device_id={"chan": partner},
        ).wait_recv()


def gathered_rows(identity, block, *swapped_arrays):
    seq_size = lax.axis_size("seq")
    chips = seq_size // 2
    swaps = len(swapped_arrays)
    dma = pltpu.SemaphoreType.DMA
    results = pl.pallas_call(
        functools.partial(ring_kernel, chips, swaps),
        out_shape=[jax.ShapeDtypeStruct((seq_size,) + block.shape, block.dtype)]
        + [jax.ShapeDtypeStruct(a.shape, a.dtype) for a in swapped_arrays],
        in_specs=[pl.BlockSpec(memory_space=pl.ANY)] * (1 + swaps),
        out_specs=[pl.BlockSpec(memory_space=pl.ANY)] * (1 + swaps),
        scratch_shapes=[
            dma((4 * (chips - 1),)),
            dma((4 * (chips - 1),)),
            dma((4 * chips,)),
            dma((4 * chips,)),
            dma,
            dma((max(swaps, 1),)),
            dma((max(swaps, 1),)),
        ],
        compiler_params=pltpu.CompilerParams(collective_id=identity, has_side_effects=True),
    )(block, *swapped_arrays)
    return results


def summed_rows(blocks, axis):
    count = lax.axis_size(axis)
    if count != 2:
        return lax.psum_scatter(blocks.astype(jnp.bfloat16), axis, scatter_dimension=0).astype(
            jnp.float32
        )
    me = lax.axis_index(axis)
    mine = lax.dynamic_index_in_dim(blocks, me, 0, keepdims=False)
    other = lax.dynamic_index_in_dim(blocks, 1 - me, 0, keepdims=False).astype(jnp.bfloat16)
    return mine + lax.ppermute(other, axis, [(0, 1), (1, 0)]).astype(jnp.float32)


def modal_filter(values, residues, rates, skip_gain):
    chan_count, seq_length = values.shape
    size = min(128, seq_length)
    count = seq_length // size
    blocks_in = values.reshape(chan_count, count, size)
    lags = jnp.arange(size, dtype=jnp.float32)
    rising = residues[:, :, None] * jnp.exp(-rates[:, :, None] * lags)
    falling = jnp.exp(rates[:, :, None] * lags)
    product = jnp.einsum("rci,rcj->cij", rising, falling, precision=lax.Precision.HIGH)
    lower = (lags[:, None] >= lags[None, :])[None]
    matrix = jnp.where(lower, product, 0.0)
    matrix = matrix + jnp.where(
        lags[:, None] == lags[None, :], skip_gain[:, None, None], 0.0
    )
    within = jnp.einsum(
        "cij,cbj->cbi", matrix.astype(jnp.bfloat16), blocks_in, preferred_element_type=jnp.float32
    )
    ending = jnp.exp(-rates[:, :, None] * (size - 1.0 - lags)).astype(jnp.bfloat16)
    ends = jnp.einsum("rcj,cbj->rbc", ending, blocks_in, preferred_element_type=jnp.float32)
    index = jnp.arange(count, dtype=jnp.float32)
    apart = index[:, None] - 1.0 - index[None, :]
    decay = jnp.where(
        (apart >= 0.0)[None, :, :, None],
        jnp.exp(-rates[:, None, None, :] * size * jnp.maximum(apart, 0.0)[None, :, :, None]),
        0.0,
    )
    entering = jnp.sum(decay * ends[:, None], axis=2)
    rise_decay = residues[:, :, None] * jnp.exp(-rates[:, :, None] * (lags + 1.0))
    before = jnp.einsum(
        "rci,rbc->cbi",
        rise_decay.astype(jnp.bfloat16),
        entering.astype(jnp.bfloat16),
        preferred_element_type=jnp.float32,
    )
    return (within + before).reshape(chan_count, seq_length)


def lagged_time(rows, weights):
    length = rows.shape[1]
    padded = jnp.concatenate([jnp.zeros_like(rows[:, :2]), rows], axis=1).astype(jnp.float32)
    running = weights[0][:, None] * padded[:, 2:]
    for lag_index in (1, 2):
        running = running + weights[lag_index][:, None] * padded[:, 2 - lag_index : 2 - lag_index + length]
    return running


def local_general(
    stream_in,
    mr_proj,
    mr_short,
    mr_filter,
    mr_out,
    li_gain,
    li_in,
    li_short,
    li_res,
    li_rate,
    li_skip,
):
    row_count = mr_proj.shape[0]
    chan_width = mr_proj.shape[2]
    tap_count = mr_filter.shape[1]
    filter_count = mr_filter.shape[0]
    seq_size = lax.axis_size("seq")
    chan_size = lax.axis_size("chan")
    width = stream_in.shape[1]
    own_count = chan_width // seq_size
    part = row_count // chan_size
    me = lax.axis_index("chan")

    out_weights = gathered_rows(1, mr_out)[0]
    out_weights, li_in, mr_proj = lax.optimization_barrier((out_weights, li_in, mr_proj))

    in_blocks = jnp.transpose(
        li_in.reshape(li_in.shape[0], 3, seq_size, own_count), (2, 0, 1, 3)
    ).reshape(seq_size, li_in.shape[0], 3 * own_count)
    pieces = scattered(in_blocks, "seq")

    rim_rows = passed_along(mr_proj[-2:], "seq", 1)
    mr_mixed = lagged_rows(
        jnp.concatenate([rim_rows, mr_proj], axis=0).astype(jnp.float32), mr_short, row_count
    )
    queries = mr_mixed[:, 0]
    own_values = (mr_mixed[:, 1] * mr_mixed[:, 2]).astype(jnp.bfloat16)
    tail_rows = passed_along(own_values[-(tap_count - 1) :], "seq", 1)
    block_count = row_count // tap_count
    padded = jnp.concatenate(
        [tail_rows, own_values, jnp.zeros((1, chan_width), jnp.bfloat16)], axis=0
    )
    columns_major = padded.T.reshape(filter_count, GROUP, block_count + 1, tap_count)
    band_matrix = band_matrices(mr_filter)
    filtered_mr = jnp.einsum(
        "gis,gcbs->gcbi",
        band_matrix[:, :, :tap_count],
        columns_major[:, :, :-1],
        preferred_element_type=jnp.float32,
    )
    filtered_mr = filtered_mr + jnp.einsum(
        "gis,gcbs->gcbi",
        band_matrix[:, :, tap_count:],
        columns_major[:, :, 1:],
        preferred_element_type=jnp.float32,
    )
    filtered_rows = filtered_mr.reshape(chan_width, row_count).T
    gated = (queries * filtered_rows).astype(jnp.bfloat16)
    branch = branch_product(gated, out_weights)
    branch, pieces = lax.optimization_barrier((branch, pieces))
    in_own = assembled(pieces, "seq").reshape(width, 3 * own_count)
    summed = summed_rows(branch.reshape(chan_size, part, width), "chan")
    own_stream = lax.dynamic_slice_in_dim(stream_in, me * part, part, 0)
    stream = (own_stream.astype(jnp.float32) + summed).astype(jnp.bfloat16)
    stream_wide = stream.astype(jnp.float32)
    inverse_rms = lax.rsqrt(jnp.mean(stream_wide * stream_wide, axis=1, keepdims=True) + EPSILON)
    normed = (stream_wide * inverse_rms * li_gain[None]).astype(jnp.bfloat16)
    stream_parts = jnp.moveaxis(stream.reshape(part, chan_size, chan_width), 1, 0)
    if chan_size == 2:
        swap = [(0, 1), (1, 0)]
        stream_mine = lax.dynamic_index_in_dim(stream_parts, me, 0, keepdims=False)
        stream_other = lax.dynamic_index_in_dim(stream_parts, 1 - me, 0, keepdims=False)
        gathered, in_other, stream_other = gathered_rows(
            0, normed, in_own, stream_other
        )
        gathered = gathered.reshape(seq_size * part, width)
        stream_out = jnp.concatenate(
            [
                jnp.where(me == 0, stream_mine, stream_other),
                jnp.where(me == 0, stream_other, stream_mine),
            ]
        )

        def product(rows, matrix, low, high):
            return jnp.dot(
                rows,
                matrix[:, low * own_count : high * own_count],
                preferred_element_type=jnp.float32,
            ).astype(jnp.bfloat16)

        outgoing = product(gathered, in_other, 1, 3)
        sent = lax.ppermute(outgoing, "chan", swap)
        later, _ = lax.optimization_barrier((gathered, outgoing))
        outgoing_opener = product(later, in_other, 0, 1)
        sent_opener = lax.ppermute(outgoing_opener, "chan", swap)
        last, _ = lax.optimization_barrier((gathered, outgoing_opener))
        kept = product(last, in_own, 0, 3)
        kept, li_rate = lax.optimization_barrier((kept, li_rate))
        received = (sent_opener, sent[:, :own_count], sent[:, own_count:])

        def ordered(index):
            mine = kept[:, index * own_count : (index + 1) * own_count].T
            theirs = received[index].T
            pair = [
                jnp.where(me == 0, mine, theirs).reshape(own_count, seq_size, 1, part),
                jnp.where(me == 0, theirs, mine).reshape(own_count, seq_size, 1, part),
            ]
            return jnp.concatenate(pair, axis=2).reshape(own_count, seq_size * row_count)
    else:
        stream_out = swapped(stream_parts, "chan").reshape(row_count, chan_width)
        gathered = gathered_rows(0, normed)[0].reshape(seq_size * part, width)
        in_all = lax.all_gather(in_own, "chan", axis=0)
        raw = jnp.einsum(
            "xdn,td->xnt", in_all, gathered, preferred_element_type=jnp.float32
        ).astype(jnp.bfloat16)
        raw = swapped(raw, "chan").reshape(chan_size, 3, own_count, seq_size, part)
        raw = jnp.transpose(raw, (1, 2, 3, 0, 4)).reshape(3, own_count, seq_size * row_count)

        def ordered(index):
            return raw[index]

    keys, gates = ordered(1), ordered(2)
    seq_offset = lax.axis_index("seq") * own_count
    own_short = lax.dynamic_slice_in_dim(li_short, seq_offset, own_count, 2)
    own_res = lax.dynamic_slice_in_dim(li_res, seq_offset, own_count, 1)
    own_rate = lax.dynamic_slice_in_dim(li_rate, seq_offset, own_count, 1)
    own_skip = lax.dynamic_slice_in_dim(li_skip, seq_offset, own_count, 0)
    values = (lagged_time(keys, own_short[1]) * lagged_time(gates, own_short[2])).astype(
        jnp.bfloat16
    )
    filtered = modal_filter(values, own_res, own_rate, own_skip)
    if chan_size == 2:
        filtered, sent_opener = lax.optimization_barrier((filtered, sent_opener))
        received = (sent_opener,) + received[1:]
    openers = ordered(0)
    result = (lagged_time(openers, own_short[0]) * filtered).astype(jnp.bfloat16)
    li_output = lax.all_to_all(result, "seq", split_axis=1, concat_axis=0, tiled=True)
    return (stream_out, li_output)


HALVES = 2
PLANE = 8
SIB, NEAR, FAR, ACROSS = 1, 2, 4, 8


def flipped(bit, flip):
    return bit + flip - 2 * bit * flip


class Place:
    def __init__(self):
        seat = lax.axis_index("seq")
        self.side = lax.axis_index("chan")
        self.half = seat // PLANE
        self.spot = lax.rem(seat, PLANE)
        self.bits = (lax.rem(self.spot, 2), lax.rem(self.spot // 2, 2), self.spot // 4)

    def spot_at(self, code):
        return sum(flipped(self.bits[i], (code >> i) & 1) << i for i in range(3))

    def pair_at(self, code):
        return flipped(self.bits[1], code & 1) + 2 * flipped(self.bits[2], (code >> 1) & 1)

    def seat_at(self, half_flip, code):
        return flipped(self.half, half_flip) * PLANE + self.spot_at(code)

    def side_at(self, code):
        return flipped(self.side, (code >> 3) & 1)

    def target(self, code):
        if code == ACROSS:
            return {"chan": 1 - self.side}
        return {"seq": self.seat_at(0, code)}


def greeted(place, seats, across):
    barrier = pltpu.get_barrier_semaphore()
    for half_flip, code in seats:
        pl.semaphore_signal(barrier, inc=1, device_id={"seq": place.seat_at(half_flip, code)})
    if across:
        pl.semaphore_signal(barrier, inc=1, device_id={"chan": 1 - place.side})
    pl.semaphore_wait(barrier, len(seats) + across)


def tapped(extended, weights, start, rows):
    total = weights[0:1] * extended[start : start + rows]
    for lag in (1, 2):
        total = total + weights[lag : lag + 1] * extended[start - lag : start - lag + rows]
    return total


def mixing_kernel(own_ref, tail_ref, rim_ref, short_ref, base_ref, out_ref):
    rows, lanes = out_ref.shape
    taps = base_ref.shape[1] // 2
    keep = tail_ref.shape[1]
    parts = []
    for p in (1, 2):
        extended = jnp.concatenate([tail_ref[p - 1], own_ref[p]], axis=0).astype(jnp.float32)
        parts.append(tapped(extended, short_ref[p], keep - taps, rows + taps))
    values = (parts[0] * parts[1]).astype(jnp.bfloat16)
    blocks = rows // taps
    operand = jnp.concatenate(
        [values[b * taps : b * taps + 2 * taps] for b in range(blocks)], axis=1
    )
    group_count = lanes // GROUP
    lane = lax.broadcasted_iota(jnp.int32, (taps, blocks * lanes), 1)
    member = lax.rem(lane, lanes) // GROUP
    picked = None
    for g in range(group_count):
        row = jnp.broadcast_to(base_ref[g : g + 1, :], (taps, 2 * taps))
        band = pltpu.roll(row, 0, 1, stride=1, stride_axis=0).astype(jnp.bfloat16)
        product = jnp.dot(band, operand, preferred_element_type=jnp.float32)
        picked = product if picked is None else jnp.where(member == g, product, picked)
    extended = jnp.concatenate([rim_ref[...], own_ref[0]], axis=0).astype(jnp.float32)
    queries = tapped(extended, short_ref[0], rim_ref.shape[0], rows)
    for b in range(blocks):
        out_ref[b * taps : (b + 1) * taps] = (
            queries[b * taps : (b + 1) * taps] * picked[:, b * lanes : (b + 1) * lanes]
        ).astype(out_ref.dtype)


def mixed_rows(proj, tail, rim, short, base):
    _, rows, width = proj.shape
    lanes = 128
    groups = lanes // GROUP
    return pl.pallas_call(
        mixing_kernel,
        out_shape=jax.ShapeDtypeStruct((rows, width), jnp.bfloat16),
        grid=(width // lanes,),
        in_specs=[
            pl.BlockSpec((3, rows, lanes), lambda i: (0, 0, i)),
            pl.BlockSpec((2, tail.shape[1], lanes), lambda i: (0, 0, i)),
            pl.BlockSpec((rim.shape[0], lanes), lambda i: (0, i)),
            pl.BlockSpec((3, 3, lanes), lambda i: (0, 0, i)),
            pl.BlockSpec((groups, base.shape[1]), lambda i: (i, 0)),
        ],
        out_specs=pl.BlockSpec((rows, lanes), lambda i: (0, i)),
        cost_estimate=pl.CostEstimate(
            flops=4 * rows * width * 2 * base.shape[1], bytes_accessed=8 * rows * width, transcendentals=0
        ),
    )(proj, tail, rim, short, base)


BATCHES = (0, 4, 4)


def plane_kernel(
    gated, own_w, other_w, stream_in, weights, spread, pieces,
    rows_all, cols, kept, outgoing, incoming, base_rows, block, held,
    load_sem, sin_send, sin_recv, gat_send, gat_recv, x_send, x_recv, a_send, a_recv,
    b_send, b_recv,
):
    place = Place()
    rows, depth = gated.shape
    part = rows // 2
    wide = own_w.shape[1]
    chans = pieces.shape[4]
    everyone = [(f, r) for f in (0, 1) for r in range(PLANE) if (f, r) != (0, 0)]
    greeted(place, everyone, 1)
    spot, half, side = place.spot, place.half, place.side
    started = []

    def go(copy):
        copy.start()
        started.append(copy)

    loads = [
        pltpu.make_async_copy(gated, rows_all.at[spot], load_sem.at[0]),
        pltpu.make_async_copy(own_w, cols.at[half], load_sem.at[1]),
        pltpu.make_async_copy(other_w, cols.at[1 - half], load_sem.at[2]),
    ]
    mine = pl.ds(pl.multiple_of(side * part, part), part)
    for f in (0, 1):
        at = pl.multiple_of((f * PLANE + spot) * wide, wide)
        loads.append(
            pltpu.make_async_copy(
                stream_in.at[mine, pl.ds(at, wide)],
                base_rows.at[spot, :, pl.ds(f * wide, wide)],
                load_sem.at[3 + f],
            )
        )
    piece_at = pl.ds(pl.multiple_of(spot * chans, chans), chans)
    loads.append(pltpu.make_async_copy(weights.at[:, :, piece_at], held, load_sem.at[5]))
    for copy in loads:
        copy.start()

    def halves(side_code):
        return pl.ds(side_code * part, part)

    def gather(dim, code, side_code, first=False):
        slot = place.spot_at(code)
        lands = rows_all.at[slot, halves(side_code)]
        index = {SIB: 0, NEAR: 1, FAR: 2}[dim]
        return pltpu.make_async_remote_copy(
            src_ref=gated.at[halves(side_code)] if first else lands,
            dst_ref=lands,
            send_sem=gat_send.at[(index * PLANE + code) * 2 + side_code],
            recv_sem=gat_recv.at[(code ^ dim) * 2 + side_code],
            device_id=place.target(dim),
        )

    def gathered(code, side_code):
        slot = place.spot_at(code)
        lands = rows_all.at[slot, halves(side_code)]
        pltpu.make_async_remote_copy(
            src_ref=lands,
            dst_ref=lands,
            send_sem=gat_send.at[0],
            recv_sem=gat_recv.at[code * 2 + side_code],
            device_id=place.target(SIB),
        ).wait_recv()

    def base_copy(code, f):
        at = pl.multiple_of((f * PLANE + place.spot_at(code)) * wide, wide)
        return pltpu.make_async_remote_copy(
            src_ref=stream_in.at[mine, pl.ds(at, wide)],
            dst_ref=base_rows.at[spot, :, pl.ds(f * wide, wide)],
            send_sem=sin_send.at[code * 2 + f],
            recv_sem=sin_recv.at[code * 2 + f],
            device_id={"seq": place.seat_at(0, code)},
        )

    def base_wait(code, f):
        lands = base_rows.at[place.spot_at(code), :, pl.ds(f * wide, wide)]
        pltpu.make_async_remote_copy(
            src_ref=lands,
            dst_ref=lands,
            send_sem=sin_send.at[0],
            recv_sem=sin_recv.at[code * 2 + f],
            device_id={"seq": place.seat_at(0, code)},
        ).wait_recv()

    def piece_copy(f, code):
        at = pl.ds(pl.multiple_of(place.spot_at(code) * chans, chans), chans)
        return pltpu.make_async_remote_copy(
            src_ref=weights.at[:, :, at],
            dst_ref=pieces.at[spot, half],
            send_sem=b_send.at[f * PLANE + code],
            recv_sem=b_recv.at[f * PLANE + code],
            device_id={"seq": place.seat_at(f, code)},
        )

    def piece_wait(f, code):
        lands = pieces.at[place.spot_at(code), flipped(half, f)]
        pltpu.make_async_remote_copy(
            src_ref=lands,
            dst_ref=lands,
            send_sem=b_send.at[0],
            recv_sem=b_recv.at[f * PLANE + code],
            device_id={"seq": place.seat_at(f, code)},
        ).wait_recv()

    waiting = [(1, r) for r in range(PLANE)] + [(0, r) for r in range(1, PLANE)]

    def release(count):
        for _ in range(min(count, len(waiting))):
            go(piece_copy(*waiting.pop(0)))

    go(gather(NEAR, 0, 0, True))
    go(gather(FAR, 0, 1, True))
    for s in (0, 1):
        go(gather(SIB, 0, s, True))
    go(gather(NEAR, 0, 1, True))
    go(gather(FAR, 0, 0, True))
    for code in range(1, PLANE):
        for f in (0, 1):
            go(base_copy(code, f))
    release(BATCHES[0])

    def pair(code):
        return pl.ds(place.pair_at(code) * 2, 2)

    def swap(k):
        return pltpu.make_async_remote_copy(
            src_ref=outgoing.at[k],
            dst_ref=incoming.at[k],
            send_sem=x_send.at[k],
            recv_sem=x_recv.at[k],
            device_id=place.target(ACROSS),
        )

    def multiply(k):
        for who in (1, 0):
            at = pl.ds(pl.multiple_of(flipped(side, who) * part, part), part)
            left = rows_all[pair(k), at, :].reshape(2 * part, depth)
            for f in (0, 1):
                product = jnp.dot(left, cols[f], preferred_element_type=jnp.float32)
                product = product.reshape(2, part, wide)
                if who:
                    outgoing[k, :, :, f * wide : (f + 1) * wide] = product.astype(outgoing.dtype)
                else:
                    kept[k, :, :, f * wide : (f + 1) * wide] = product
            if who:
                go(swap(k))

    def spread_slot(code, k):
        return spread.at[
            place.spot_at(code & 7), pair(((code >> 1) & 3) ^ k), place.side_at(code)
        ]

    def scatter(dim, code, k):
        index = {SIB: 0, NEAR: 1, FAR: 2, ACROSS: 3}[dim]
        lands = spread_slot(code, k)
        return pltpu.make_async_remote_copy(
            src_ref=block.at[k] if code == 0 else lands,
            dst_ref=lands,
            send_sem=a_send.at[(index * 16 + code) * 4 + k],
            recv_sem=a_recv.at[(code ^ dim) * 4 + k],
            device_id=place.target(dim),
        )

    def scattered_wait(code, k):
        lands = spread_slot(code, k)
        pltpu.make_async_remote_copy(
            src_ref=lands,
            dst_ref=lands,
            send_sem=a_send.at[0],
            recv_sem=a_recv.at[code * 4 + k],
            device_id=place.target(SIB),
        ).wait_recv()

    def finish(k):
        swap(k).wait_recv()
        for code in (2 * k, 2 * k + 1):
            for f in (0, 1):
                if code:
                    base_wait(code, f)
        total = base_rows[pair(k)].astype(jnp.float32) + kept[k] + incoming[k].astype(jnp.float32)
        block[k] = total.astype(block.dtype)
        copy = pltpu.make_async_copy(block.at[k], spread_slot(0, k), load_sem.at[7 + k])
        copy.start()
        loads.append(copy)
        for dim in (FAR, NEAR, ACROSS, SIB):
            go(scatter(dim, 0, k))

    def onward(code, k):
        scattered_wait(code, k)
        if code & SIB:
            return
        order = (FAR, NEAR, ACROSS) if k != 3 else (FAR, ACROSS, NEAR)
        last = max(i for i, dim in enumerate(order) if code & dim)
        for dim in order[last + 1 :]:
            go(scatter(dim, code, k))
        go(scatter(SIB, code, k))

    for copy in loads:
        copy.wait()
    own_piece = pltpu.make_async_copy(held, pieces.at[spot, half], load_sem.at[6])
    own_piece.start()
    loads = [own_piece]
    for s in (0, 1):
        gathered(SIB, s)
    multiply(0)
    gathered(NEAR, 0)
    go(gather(FAR, NEAR, 0))
    go(gather(SIB, NEAR, 0))
    gathered(FAR, 1)
    go(gather(NEAR, FAR, 1))
    go(gather(SIB, FAR, 1))
    release(BATCHES[1])
    finish(0)
    gathered(NEAR, 1)
    go(gather(SIB, NEAR, 1))
    gathered(FAR, 0)
    go(gather(SIB, FAR, 0))
    for s in (0, 1):
        gathered(NEAR | SIB, s)
    multiply(1)
    for s in (0, 1):
        gathered(FAR | SIB, s)
    multiply(2)
    onward(FAR, 0)
    finish(1)
    for s in (0, 1):
        gathered(NEAR | FAR, s)
        go(gather(SIB, NEAR | FAR, s))
    finish(2)
    for s in (0, 1):
        gathered(NEAR | FAR | SIB, s)
    multiply(3)
    onward(NEAR, 0)
    onward(FAR, 1)
    onward(FAR, 2)
    release(BATCHES[2])
    finish(3)
    onward(NEAR | FAR, 0)
    onward(NEAR, 1)
    onward(NEAR, 2)
    onward(FAR, 3)
    release(PLANE * 2)
    onward(NEAR | FAR, 1)
    onward(NEAR | FAR, 2)
    for k in range(3):
        for code in (8, 12, 10, 14):
            onward(code, k)
    for code in (8, 12, 2, 6, 10, 14):
        onward(code, 3)
    for k in range(4):
        for code in range(1, 16, 2):
            onward(code, k)
    for f, code in everyone:
        piece_wait(f, code)
    for copy in loads:
        copy.wait()
    for copy in started:
        copy.wait_send()


def plane_exchange(gated, own_w, other_w, stream_in, weights):
    rows, depth = gated.shape
    part = rows // 2
    wide = own_w.shape[1]
    chans = weights.shape[2] // PLANE
    deep = weights.shape[1]
    dma = pltpu.SemaphoreType.DMA
    anywhere = pl.BlockSpec(memory_space=pl.ANY)
    half_block = (4, 2, part, HALVES * wide)
    return pl.pallas_call(
        plane_kernel,
        out_shape=[
            jax.ShapeDtypeStruct((PLANE, PLANE, 2, part, HALVES * wide), jnp.bfloat16),
            jax.ShapeDtypeStruct((PLANE, HALVES, 3, deep, chans), jnp.bfloat16),
        ],
        in_specs=[anywhere] * 5,
        out_specs=[anywhere] * 2,
        scratch_shapes=[
            pltpu.VMEM((PLANE, rows, depth), jnp.bfloat16),
            pltpu.VMEM((HALVES, depth, wide), jnp.bfloat16),
            pltpu.VMEM(half_block, jnp.float32),
            pltpu.VMEM(half_block, jnp.bfloat16),
            pltpu.VMEM(half_block, jnp.bfloat16),
            pltpu.VMEM((PLANE, part, HALVES * wide), jnp.bfloat16),
            pltpu.VMEM(half_block, jnp.bfloat16),
            pltpu.VMEM((3, deep, chans), jnp.bfloat16),
            dma((11,)),
            dma((2 * PLANE,)),
            dma((2 * PLANE,)),
            dma((3 * PLANE * 2,)),
            dma((PLANE * 2,)),
            dma((4,)),
            dma((4,)),
            dma((4 * 16 * 4,)),
            dma((16 * 4,)),
            dma((2 * PLANE,)),
            dma((2 * PLANE,)),
        ],
        compiler_params=pltpu.CompilerParams(
            collective_id=2, has_side_effects=True, vmem_limit_bytes=40 * 1024 * 1024
        ),
    )(gated, own_w, other_w, stream_in, weights)


RIM = 16


def filter_kernel(
    spread, pieces, short_ref, res_ref, rate_ref, skip_ref, stream_ref, out_ref,
    rows_in, matrix, proj, rim, values, openers, partial, ends, starts, state_out, state_in, turned,
    load_sem, piece_sem, stream_sem, rim_sem, state_sem, out_send, out_recv,
):
    place = Place()
    spot, half, side = place.spot, place.half, place.side
    rows = 2 * spread.shape[3]
    wide = spread.shape[4] // HALVES
    depth = PLANE * HALVES * wide
    chans = pieces.shape[4]
    lanes = 128
    groups = chans // lanes
    modes = res_ref.shape[0]
    peers = [(0, r) for r in range(1, PLANE)] + [(1, 0)]
    whole = pltpu.make_async_copy(pieces, matrix, piece_sem)
    whole.start()

    def rows_copy(slot, buffer):
        return pltpu.make_async_copy(spread.at[:, slot], rows_in.at[buffer], load_sem.at[buffer])

    rows_copy(PLANE - 1, 0).start()
    rows_copy(0, 1).start()
    greeted(place, peers, 0)
    stream_copies = []
    for other in range(PLANE):
        copy = pltpu.make_async_copy(
            spread.at[other, spot, :, :, pl.ds(pl.multiple_of(side * wide, wide), wide)],
            stream_ref.at[:, :, pl.ds(other * wide, wide)],
            stream_sem.at[other],
        )
        copy.start()
        stream_copies.append(copy)
    whole.wait()

    def product(slot, buffer):
        rows_copy(slot, buffer).wait()
        blocks = [rows_in[buffer, other].reshape(rows, HALVES * wide) for other in range(PLANE)]
        squares = None
        for piece in blocks:
            wide_piece = piece.astype(jnp.float32)
            for at in range(0, HALVES * wide, lanes):
                term = wide_piece[:, at : at + lanes] * wide_piece[:, at : at + lanes]
                squares = term if squares is None else squares + term
        mean = jnp.sum(squares, axis=1, keepdims=True) / depth
        inverse = lax.rsqrt(mean + EPSILON)
        left = jnp.concatenate(blocks, axis=1)
        at = pl.ds(pl.multiple_of(RIM + slot * rows, RIM), rows)
        for p in range(3):
            right = matrix[:, :, p].reshape(depth, chans)
            raw = jnp.dot(left, right, preferred_element_type=jnp.float32)
            proj[p, at, :] = (raw * inverse).astype(jnp.bfloat16).astype(jnp.float32)

    def rim_copy():
        return pltpu.make_async_remote_copy(
            src_ref=proj.at[:, pl.ds(PLANE * rows, RIM)],
            dst_ref=rim,
            send_sem=rim_sem.at[0],
            recv_sem=rim_sem.at[1],
            device_id={"seq": place.seat_at(1, 0)},
        )

    product(PLANE - 1, 0)
    rows_copy(1, 0).start()

    def body(i, carry):
        buffer = lax.rem(i + 1, 2)
        product(i, buffer)

        @pl.when(i + 2 < PLANE - 1)
        def _():
            rows_copy(i + 2, buffer).start()

        return carry

    product(0, 1)
    rim_copy().start()
    rows_copy(2, 1).start()
    lax.fori_loop(1, PLANE - 1, body, 0)
    rim_copy().wait()
    later = (half > 0).astype(jnp.float32)
    proj[:, 0:RIM, :] = rim[...] * later
    chan_at = pl.ds(pl.multiple_of(spot * chans, chans), chans)
    for slot in range(PLANE):
        mixed = []
        for p in range(3):
            weights = short_ref[p, :, chan_at]
            start = RIM + slot * rows
            total = weights[0:1] * proj[p, start : start + rows, :]
            for lag in (1, 2):
                total = total + weights[lag : lag + 1] * proj[p, start - lag : start - lag + rows, :]
            mixed.append(total)
        value = (mixed[1] * mixed[2]).astype(jnp.bfloat16).astype(jnp.float32)
        for group in range(groups):
            at = slice(group * lanes, (group + 1) * lanes)
            openers[group, slot * rows : (slot + 1) * rows, :] = mixed[0][:, at]
            values[group, slot * rows : (slot + 1) * rows, :] = value[:, at]

    def laned(ref, row, group):
        at = pl.ds(pl.multiple_of(spot * chans + group * lanes, lanes), lanes)
        return ref[row : row + 1, at]

    for group in range(groups):
        at = slice(group * lanes, (group + 1) * lanes)
        decays = [
            jnp.broadcast_to(jnp.exp(-laned(rate_ref, r, group)), (PLANE, lanes))
            for r in range(modes)
        ]
        gains = [jnp.broadcast_to(laned(res_ref, r, group), (PLANE, lanes)) for r in range(modes)]

        def step(t, states):
            value = values[group, pl.ds(t, PLANE, stride=rows), :]
            states = tuple(d * s + value for d, s in zip(decays, states))
            terms = [g * s for g, s in zip(gains, states)]
            while len(terms) > 1:
                terms = [a + b for a, b in zip(terms[::2], terms[1::2])]
            partial[group, pl.ds(t, PLANE, stride=rows), :] = terms[0]
            return states

        states = lax.fori_loop(
            0, rows, step, tuple(jnp.zeros((PLANE, lanes), jnp.float32) for _ in range(modes)), unroll=4
        )
        for r in range(modes):
            ends[:, r, at] = states[r]

    leap = jnp.exp(-rate_ref[:, chan_at] * rows)
    total = jnp.zeros((modes, chans), jnp.float32)
    for slot in range(PLANE):
        total = leap * total + ends[slot]
    state_out[...] = total
    state_copy = pltpu.make_async_remote_copy(
        src_ref=state_out,
        dst_ref=state_in,
        send_sem=state_sem.at[0],
        recv_sem=state_sem.at[1],
        device_id={"seq": place.seat_at(1, 0)},
    )
    state_copy.start()
    state_copy.wait()
    total = state_in[...] * later
    opening = res_ref[:, chan_at] * jnp.exp(-rate_ref[:, chan_at])
    for slot in range(PLANE):
        for r in range(modes):
            starts[r, slot : slot + 1, :] = (opening * total)[r : r + 1]
        total = leap * total + ends[slot]

    for group in range(groups):
        at = slice(group * lanes, (group + 1) * lanes)
        decays = [
            jnp.broadcast_to(jnp.exp(-laned(rate_ref, r, group)), (PLANE, lanes))
            for r in range(modes)
        ]
        skip = jnp.broadcast_to(laned(skip_ref, 0, group), (PLANE, lanes))

        def finish(t, states):
            where = pl.ds(t, PLANE, stride=rows)
            terms = list(states) + [partial[group, where, :], skip * values[group, where, :]]
            while len(terms) > 1:
                odd = terms[-1:] if len(terms) % 2 else []
                terms = [a + b for a, b in zip(terms[::2], terms[1::2])] + odd
            partial[group, where, :] = openers[group, where, :] * terms[0]
            return tuple(d * s for d, s in zip(decays, states))

        lax.fori_loop(0, rows, finish, tuple(starts[r, :, at] for r in range(modes)), unroll=4)

    sent = []
    mine = pl.ds(pl.multiple_of(spot * chans, chans), chans)
    for code in list(range(1, PLANE)) + [0]:
        where = pl.ds(pl.multiple_of(place.spot_at(code) * rows, rows), rows)
        for group in range(groups):
            turned[code, group * lanes : (group + 1) * lanes, :] = partial[group, where, :].T.astype(
                turned.dtype
            )
        if code:
            copy = pltpu.make_async_remote_copy(
                src_ref=turned.at[code],
                dst_ref=out_ref.at[mine],
                send_sem=out_send.at[code],
                recv_sem=out_recv.at[code],
                device_id={"seq": place.seat_at(0, code)},
            )
        else:
            copy = pltpu.make_async_copy(turned.at[0], out_ref.at[mine], out_send.at[0])
        copy.start()
        sent.append(copy)
    sent[-1].wait()
    for code in range(1, PLANE):
        lands = out_ref.at[pl.ds(pl.multiple_of(place.spot_at(code) * chans, chans), chans)]
        pltpu.make_async_remote_copy(
            src_ref=turned.at[code],
            dst_ref=lands,
            send_sem=out_send.at[code],
            recv_sem=out_recv.at[code],
            device_id={"seq": place.seat_at(0, code)},
        ).wait_recv()
        sent[code - 1].wait_send()
    for copy in stream_copies:
        copy.wait()


def filtered_rows(spread, pieces, short, residues, rates, skip):
    part = spread.shape[3]
    rows = 2 * part
    wide = spread.shape[4] // HALVES
    chans = pieces.shape[4]
    modes = residues.shape[0]
    length = PLANE * rows
    dma = pltpu.SemaphoreType.DMA
    anywhere = pl.BlockSpec(memory_space=pl.ANY)
    local_memory = pl.BlockSpec(memory_space=pltpu.VMEM)
    return pl.pallas_call(
        filter_kernel,
        out_shape=[
            jax.ShapeDtypeStruct((2, part, PLANE * wide), jnp.bfloat16),
            jax.ShapeDtypeStruct((PLANE * chans, rows), jnp.bfloat16),
        ],
        in_specs=[anywhere] * 2 + [local_memory] * 4,
        out_specs=[local_memory, anywhere],
        scratch_shapes=[
            pltpu.VMEM((2, PLANE, 2, part, HALVES * wide), jnp.bfloat16),
            pltpu.VMEM(pieces.shape, jnp.bfloat16),
            pltpu.VMEM((3, RIM + length, chans), jnp.float32),
            pltpu.VMEM((3, RIM, chans), jnp.float32),
            pltpu.VMEM((chans // 128, length, 128), jnp.float32),
            pltpu.VMEM((chans // 128, length, 128), jnp.float32),
            pltpu.VMEM((chans // 128, length, 128), jnp.float32),
            pltpu.VMEM((PLANE, modes, chans), jnp.float32),
            pltpu.VMEM((modes, PLANE, chans), jnp.float32),
            pltpu.VMEM((modes, chans), jnp.float32),
            pltpu.VMEM((modes, chans), jnp.float32),
            pltpu.VMEM((PLANE, chans, rows), jnp.bfloat16),
            dma((2,)),
            dma,
            dma((PLANE,)),
            dma((2,)),
            dma((2,)),
            dma((PLANE,)),
            dma((PLANE,)),
        ],
        compiler_params=pltpu.CompilerParams(
            collective_id=3, has_side_effects=True, vmem_limit_bytes=56 * 1024 * 1024
        ),
    )(spread, pieces, short, residues, rates, skip)


def local_halves(
    stream_in,
    mr_proj,
    mr_short,
    mr_filter,
    mr_out,
    li_gain,
    li_in,
    li_short,
    li_res,
    li_rate,
    li_skip,
):
    seq_size = lax.axis_size("seq")
    row_count, _, width = mr_proj.shape
    taps = mr_filter.shape[1]
    seat = lax.axis_index("seq")
    proj = jnp.transpose(mr_proj, (1, 0, 2))
    tail = passed_along(proj[1:, -(taps + RIM) :], "seq", 1)
    rim = passed_along(proj[0, -RIM:], "seq", 1)
    other_w = lax.ppermute(
        mr_out, "seq", [(i, (i + PLANE) % seq_size) for i in range(seq_size)]
    )
    gain = lax.dynamic_slice_in_dim(li_gain, seat * li_in.shape[0], li_in.shape[0], 0)
    weights = (jnp.transpose(li_in, (1, 0, 2)) * gain[None, :, None]).astype(jnp.bfloat16)
    base = jnp.pad(mr_filter[:, ::-1], ((0, 0), (1, taps - 1)))
    gated = mixed_rows(proj, tail, rim, mr_short, base)
    spread, pieces = plane_exchange(gated, mr_out, other_w, stream_in, weights)
    stream, filtered = filtered_rows(
        spread, pieces, li_short, li_res, li_rate, li_skip[None]
    )
    return stream.reshape(row_count, width), filtered


def local(*arrays):
    halves = lax.axis_size("chan") == 2 and lax.axis_size("seq") == HALVES * PLANE
    return (local_halves if halves else local_general)(*arrays)


def solution(mesh):
    in_specs = (
        P("seq", None),
        P("seq", None, "chan"),
        P(None, None, "chan"),
        P("chan", None),
        P("chan", "seq"),
        P(),
        P("seq", None, "chan"),
        P(None, None, "chan"),
        P(None, "chan"),
        P(None, "chan"),
        P("chan"),
    )
    out_specs = (P("seq", "chan"), P("chan", "seq"))
    return jax.shard_map(local, mesh=mesh, in_specs=in_specs, out_specs=out_specs, check_vma=False)
```

```python
import functools

import jax
import jax.numpy as jnp
from jax import lax
from jax.experimental import pallas as pl
from jax.experimental.pallas import tpu as pltpu
from jax.sharding import PartitionSpec as P

GROUP = 16


EPSILON = 1e-06
HIGHEST = lax.Precision.HIGHEST


def passed_along(block, axis, distance):
    devices = range(lax.axis_size(axis))
    route = [(i - distance, i) for i in devices if i - distance in devices]
    return lax.ppermute(block, axis, route)


def band_matrices(filters):
    tap_count = filters.shape[1]
    out_index = jnp.arange(tap_count, dtype=jnp.int32)[:, None, None]
    in_index = jnp.arange(2 * tap_count, dtype=jnp.int32)[None, :, None]
    lag_index = jnp.arange(tap_count, dtype=jnp.int32)[None, None, :]
    selector = (out_index + tap_count - 1 - in_index == lag_index).astype(jnp.bfloat16)
    return jnp.einsum(
        "gj,isj->gis", filters.astype(jnp.bfloat16), selector, preferred_element_type=jnp.float32
    ).astype(jnp.bfloat16)


def lagged_rows(extended, weights, row_count):
    running = weights[:, 0][None] * extended[2 : 2 + row_count]
    for lag_index in (1, 2):
        running = (
            running
            + weights[:, lag_index][None] * extended[2 - lag_index : 2 - lag_index + row_count]
        )
    return running


def swapped(blocks, axis):
    count = lax.axis_size(axis)
    if count != 2:
        return lax.all_to_all(blocks, axis, split_axis=0, concat_axis=0, tiled=True)
    me = lax.axis_index(axis)
    mine = lax.dynamic_index_in_dim(blocks, me, 0, keepdims=False)
    other = lax.dynamic_index_in_dim(blocks, 1 - me, 0, keepdims=False)
    received = lax.ppermute(other, axis, [(0, 1), (1, 0)])
    first = me == 0
    return jnp.stack([jnp.where(first, mine, received), jnp.where(first, received, mine)])


def scattered(blocks, axis):
    count = lax.axis_size(axis)
    me = lax.axis_index(axis)
    chips, chip = count // 2, me // 2
    pairs = blocks.reshape((chips, 2) + blocks.shape[1:])
    pieces = []
    for k in range(chips):
        piece = lax.dynamic_index_in_dim(pairs, lax.rem(chip + k, chips), 0, keepdims=False)
        if k:
            route = [(i, (i + 2 * k) % count) for i in range(count)]
            piece = lax.ppermute(piece, axis, route)
        pieces.append(piece)
    return pieces


def assembled(pieces, axis):
    count = lax.axis_size(axis)
    me = lax.axis_index(axis)
    chips, chip, core = count // 2, me // 2, lax.rem(me, 2)
    kept = jnp.stack([lax.dynamic_index_in_dim(p, core, 0, keepdims=False) for p in pieces])
    given = jnp.stack([lax.dynamic_index_in_dim(p, 1 - core, 0, keepdims=False) for p in pieces])
    taken = lax.ppermute(given, axis, [(i, i ^ 1) for i in range(count)])
    both = jnp.stack(
        [jnp.where(core == 0, kept, taken), jnp.where(core == 0, taken, kept)], axis=1
    )
    both = both[::-1]
    return lax.dynamic_slice_in_dim(
        jnp.concatenate([both, both]), lax.rem(2 * chips - 1 - chip, chips), chips, 0
    )


def branch_kernel(gated_ref, weights_ref, out_ref):
    out_ref[...] = jnp.dot(gated_ref[...], weights_ref[0], preferred_element_type=jnp.float32)


def branch_product(gated, weights):
    rows, depth = gated.shape
    blocks, _, columns = weights.shape
    return pl.pallas_call(
        branch_kernel,
        out_shape=jax.ShapeDtypeStruct((rows, blocks * columns), jnp.float32),
        grid=(blocks,),
        in_specs=[
            pl.BlockSpec((rows, depth), lambda i: (0, 0)),
            pl.BlockSpec((1, depth, columns), lambda i: (i, 0, 0)),
        ],
        out_specs=pl.BlockSpec((rows, columns), lambda i: (0, i)),
        cost_estimate=pl.CostEstimate(
            flops=2 * rows * depth * blocks * columns,
            bytes_accessed=2 * blocks * depth * columns,
            transcendentals=0,
        ),
    )(gated, weights)


PARTS = 4


def ring_kernel(chips, swaps, *refs):
    inputs, outputs, sems = refs[: 1 + swaps], refs[1 + swaps : 2 + 2 * swaps], refs[2 + 2 * swaps :]
    block_ref, out_ref = inputs[0], outputs[0]
    ring_send, ring_recv, core_send, core_recv, own_sem, swap_send, swap_recv = sems
    me = lax.axis_index("seq")
    core = lax.rem(me, 2)
    chip = me // 2
    row, column = chip // 2, lax.rem(chip, 2)
    place = row + column * (chips - 1 - 2 * row)
    sibling = me + 1 - 2 * core
    rows = block_ref.shape[0] // PARTS

    def device(position, core_index):
        position = lax.rem(position + 2 * chips, chips)
        second = position // (chips // 2)
        at_row = position + second * (chips - 1 - 2 * position)
        return (2 * at_row + second) * 2 + core_index

    following, preceding = device(place + 1, core), device(place - 1, core)
    barrier = pltpu.get_barrier_semaphore()
    for target in (following, preceding, sibling):
        pl.semaphore_signal(barrier, inc=1, device_id={"seq": target})
    if swaps:
        partner = 1 - lax.axis_index("chan")
        pl.semaphore_signal(barrier, inc=1, device_id={"chan": partner})
    pl.semaphore_wait(barrier, 4 if swaps else 3)

    def ring(way, step, half, source, slot):
        part = pl.ds((2 * way + half) * rows, rows)
        index = (way * (chips - 1) + step) * 2 + half
        return pltpu.make_async_remote_copy(
            src_ref=source.at[part],
            dst_ref=out_ref.at[slot, part],
            send_sem=ring_send.at[index],
            recv_sem=ring_recv.at[index],
            device_id={"seq": (following, preceding)[way]},
        )

    def across(way, step, half, source, slot):
        part = pl.ds((2 * way + half) * rows, rows)
        index = (way * chips + step) * 2 + half
        return pltpu.make_async_remote_copy(
            src_ref=source.at[part],
            dst_ref=out_ref.at[slot, part],
            send_sem=core_send.at[index],
            recv_sem=core_recv.at[index],
            device_id={"seq": sibling},
        )

    started = []
    for step in range(chips):
        for half in (0, 1):
            for way in (0, 1):
                slot = device(place + (2 * way - 1) * step, core)
                source = block_ref if step == 0 else out_ref.at[slot]
                if step:
                    ring(way, step - 1, half, source, slot).wait_recv()
                if step < chips - 1:
                    copy = ring(way, step, half, source, slot)
                    copy.start()
                    started.append(copy)
                copy = across(way, step, half, source, slot)
                copy.start()
                started.append(copy)
        if step == 0:
            for i in range(swaps):
                copy = pltpu.make_async_remote_copy(
                    src_ref=inputs[1 + i],
                    dst_ref=outputs[1 + i],
                    send_sem=swap_send.at[i],
                    recv_sem=swap_recv.at[i],
                    device_id={"chan": partner},
                )
                copy.start()
                started.append(copy)
            own = pltpu.make_async_copy(block_ref, out_ref.at[me], own_sem)
            own.start()
    for step in range(chips):
        for half in (0, 1):
            for way in (0, 1):
                slot = device(place + (2 * way - 1) * step, 1 - core)
                across(way, step, half, out_ref.at[slot], slot).wait_recv()
    own.wait()
    for copy in started:
        copy.wait_send()
    for i in range(swaps):
        pltpu.make_async_remote_copy(
            src_ref=inputs[1 + i],
            dst_ref=outputs[1 + i],
            send_sem=swap_send.at[i],
            recv_sem=swap_recv.at[i],
            device_id={"chan": partner},
        ).wait_recv()


def gathered_rows(identity, block, *swapped_arrays):
    seq_size = lax.axis_size("seq")
    chips = seq_size // 2
    swaps = len(swapped_arrays)
    dma = pltpu.SemaphoreType.DMA
    results = pl.pallas_call(
        functools.partial(ring_kernel, chips, swaps),
        out_shape=[jax.ShapeDtypeStruct((seq_size,) + block.shape, block.dtype)]
        + [jax.ShapeDtypeStruct(a.shape, a.dtype) for a in swapped_arrays],
        in_specs=[pl.BlockSpec(memory_space=pl.ANY)] * (1 + swaps),
        out_specs=[pl.BlockSpec(memory_space=pl.ANY)] * (1 + swaps),
        scratch_shapes=[
            dma((4 * (chips - 1),)),
            dma((4 * (chips - 1),)),
            dma((4 * chips,)),
            dma((4 * chips,)),
            dma,
            dma((max(swaps, 1),)),
            dma((max(swaps, 1),)),
        ],
        compiler_params=pltpu.CompilerParams(collective_id=identity, has_side_effects=True),
    )(block, *swapped_arrays)
    return results


def summed_rows(blocks, axis):
    count = lax.axis_size(axis)
    if count != 2:
        return lax.psum_scatter(blocks.astype(jnp.bfloat16), axis, scatter_dimension=0).astype(
            jnp.float32
        )
    me = lax.axis_index(axis)
    mine = lax.dynamic_index_in_dim(blocks, me, 0, keepdims=False)
    other = lax.dynamic_index_in_dim(blocks, 1 - me, 0, keepdims=False).astype(jnp.bfloat16)
    return mine + lax.ppermute(other, axis, [(0, 1), (1, 0)]).astype(jnp.float32)


def modal_filter(values, residues, rates, skip_gain):
    chan_count, seq_length = values.shape
    size = min(128, seq_length)
    count = seq_length // size
    blocks_in = values.reshape(chan_count, count, size)
    lags = jnp.arange(size, dtype=jnp.float32)
    rising = residues[:, :, None] * jnp.exp(-rates[:, :, None] * lags)
    falling = jnp.exp(rates[:, :, None] * lags)
    product = jnp.einsum("rci,rcj->cij", rising, falling, precision=lax.Precision.HIGH)
    lower = (lags[:, None] >= lags[None, :])[None]
    matrix = jnp.where(lower, product, 0.0)
    matrix = matrix + jnp.where(
        lags[:, None] == lags[None, :], skip_gain[:, None, None], 0.0
    )
    within = jnp.einsum(
        "cij,cbj->cbi", matrix.astype(jnp.bfloat16), blocks_in, preferred_element_type=jnp.float32
    )
    ending = jnp.exp(-rates[:, :, None] * (size - 1.0 - lags)).astype(jnp.bfloat16)
    ends = jnp.einsum("rcj,cbj->rbc", ending, blocks_in, preferred_element_type=jnp.float32)
    index = jnp.arange(count, dtype=jnp.float32)
    apart = index[:, None] - 1.0 - index[None, :]
    decay = jnp.where(
        (apart >= 0.0)[None, :, :, None],
        jnp.exp(-rates[:, None, None, :] * size * jnp.maximum(apart, 0.0)[None, :, :, None]),
        0.0,
    )
    entering = jnp.sum(decay * ends[:, None], axis=2)
    rise_decay = residues[:, :, None] * jnp.exp(-rates[:, :, None] * (lags + 1.0))
    before = jnp.einsum(
        "rci,rbc->cbi",
        rise_decay.astype(jnp.bfloat16),
        entering.astype(jnp.bfloat16),
        preferred_element_type=jnp.float32,
    )
    return (within + before).reshape(chan_count, seq_length)


def lagged_time(rows, weights):
    length = rows.shape[1]
    padded = jnp.concatenate([jnp.zeros_like(rows[:, :2]), rows], axis=1).astype(jnp.float32)
    running = weights[0][:, None] * padded[:, 2:]
    for lag_index in (1, 2):
        running = running + weights[lag_index][:, None] * padded[:, 2 - lag_index : 2 - lag_index + length]
    return running


def local_general(
    stream_in,
    mr_proj,
    mr_short,
    mr_filter,
    mr_out,
    li_gain,
    li_in,
    li_short,
    li_res,
    li_rate,
    li_skip,
):
    row_count = mr_proj.shape[0]
    chan_width = mr_proj.shape[2]
    tap_count = mr_filter.shape[1]
    filter_count = mr_filter.shape[0]
    seq_size = lax.axis_size("seq")
    chan_size = lax.axis_size("chan")
    width = stream_in.shape[1]
    own_count = chan_width // seq_size
    part = row_count // chan_size
    me = lax.axis_index("chan")

    out_weights = gathered_rows(1, mr_out)[0]
    out_weights, li_in, mr_proj = lax.optimization_barrier((out_weights, li_in, mr_proj))

    in_blocks = jnp.transpose(
        li_in.reshape(li_in.shape[0], 3, seq_size, own_count), (2, 0, 1, 3)
    ).reshape(seq_size, li_in.shape[0], 3 * own_count)
    pieces = scattered(in_blocks, "seq")

    rim_rows = passed_along(mr_proj[-2:], "seq", 1)
    mr_mixed = lagged_rows(
        jnp.concatenate([rim_rows, mr_proj], axis=0).astype(jnp.float32), mr_short, row_count
    )
    queries = mr_mixed[:, 0]
    own_values = (mr_mixed[:, 1] * mr_mixed[:, 2]).astype(jnp.bfloat16)
    tail_rows = passed_along(own_values[-(tap_count - 1) :], "seq", 1)
    block_count = row_count // tap_count
    padded = jnp.concatenate(
        [tail_rows, own_values, jnp.zeros((1, chan_width), jnp.bfloat16)], axis=0
    )
    columns_major = padded.T.reshape(filter_count, GROUP, block_count + 1, tap_count)
    band_matrix = band_matrices(mr_filter)
    filtered_mr = jnp.einsum(
        "gis,gcbs->gcbi",
        band_matrix[:, :, :tap_count],
        columns_major[:, :, :-1],
        preferred_element_type=jnp.float32,
    )
    filtered_mr = filtered_mr + jnp.einsum(
        "gis,gcbs->gcbi",
        band_matrix[:, :, tap_count:],
        columns_major[:, :, 1:],
        preferred_element_type=jnp.float32,
    )
    filtered_rows = filtered_mr.reshape(chan_width, row_count).T
    gated = (queries * filtered_rows).astype(jnp.bfloat16)
    branch = branch_product(gated, out_weights)
    branch, pieces = lax.optimization_barrier((branch, pieces))
    in_own = assembled(pieces, "seq").reshape(width, 3 * own_count)
    summed = summed_rows(branch.reshape(chan_size, part, width), "chan")
    own_stream = lax.dynamic_slice_in_dim(stream_in, me * part, part, 0)
    stream = (own_stream.astype(jnp.float32) + summed).astype(jnp.bfloat16)
    stream_wide = stream.astype(jnp.float32)
    inverse_rms = lax.rsqrt(jnp.mean(stream_wide * stream_wide, axis=1, keepdims=True) + EPSILON)
    normed = (stream_wide * inverse_rms * li_gain[None]).astype(jnp.bfloat16)
    stream_parts = jnp.moveaxis(stream.reshape(part, chan_size, chan_width), 1, 0)
    if chan_size == 2:
        swap = [(0, 1), (1, 0)]
        stream_mine = lax.dynamic_index_in_dim(stream_parts, me, 0, keepdims=False)
        stream_other = lax.dynamic_index_in_dim(stream_parts, 1 - me, 0, keepdims=False)
        gathered, in_other, stream_other = gathered_rows(
            0, normed, in_own, stream_other
        )
        gathered = gathered.reshape(seq_size * part, width)
        stream_out = jnp.concatenate(
            [
                jnp.where(me == 0, stream_mine, stream_other),
                jnp.where(me == 0, stream_other, stream_mine),
            ]
        )

        def product(rows, matrix, low, high):
            return jnp.dot(
                rows,
                matrix[:, low * own_count : high * own_count],
                preferred_element_type=jnp.float32,
            ).astype(jnp.bfloat16)

        outgoing = product(gathered, in_other, 1, 3)
        sent = lax.ppermute(outgoing, "chan", swap)
        later, _ = lax.optimization_barrier((gathered, outgoing))
        outgoing_opener = product(later, in_other, 0, 1)
        sent_opener = lax.ppermute(outgoing_opener, "chan", swap)
        last, _ = lax.optimization_barrier((gathered, outgoing_opener))
        kept = product(last, in_own, 0, 3)
        kept, li_rate = lax.optimization_barrier((kept, li_rate))
        received = (sent_opener, sent[:, :own_count], sent[:, own_count:])

        def ordered(index):
            mine = kept[:, index * own_count : (index + 1) * own_count].T
            theirs = received[index].T
            pair = [
                jnp.where(me == 0, mine, theirs).reshape(own_count, seq_size, 1, part),
                jnp.where(me == 0, theirs, mine).reshape(own_count, seq_size, 1, part),
            ]
            return jnp.concatenate(pair, axis=2).reshape(own_count, seq_size * row_count)
    else:
        stream_out = swapped(stream_parts, "chan").reshape(row_count, chan_width)
        gathered = gathered_rows(0, normed)[0].reshape(seq_size * part, width)
        in_all = lax.all_gather(in_own, "chan", axis=0)
        raw = jnp.einsum(
            "xdn,td->xnt", in_all, gathered, preferred_element_type=jnp.float32
        ).astype(jnp.bfloat16)
        raw = swapped(raw, "chan").reshape(chan_size, 3, own_count, seq_size, part)
        raw = jnp.transpose(raw, (1, 2, 3, 0, 4)).reshape(3, own_count, seq_size * row_count)

        def ordered(index):
            return raw[index]

    keys, gates = ordered(1), ordered(2)
    seq_offset = lax.axis_index("seq") * own_count
    own_short = lax.dynamic_slice_in_dim(li_short, seq_offset, own_count, 2)
    own_res = lax.dynamic_slice_in_dim(li_res, seq_offset, own_count, 1)
    own_rate = lax.dynamic_slice_in_dim(li_rate, seq_offset, own_count, 1)
    own_skip = lax.dynamic_slice_in_dim(li_skip, seq_offset, own_count, 0)
    values = (lagged_time(keys, own_short[1]) * lagged_time(gates, own_short[2])).astype(
        jnp.bfloat16
    )
    filtered = modal_filter(values, own_res, own_rate, own_skip)
    if chan_size == 2:
        filtered, sent_opener = lax.optimization_barrier((filtered, sent_opener))
        received = (sent_opener,) + received[1:]
    openers = ordered(0)
    result = (lagged_time(openers, own_short[0]) * filtered).astype(jnp.bfloat16)
    li_output = lax.all_to_all(result, "seq", split_axis=1, concat_axis=0, tiled=True)
    return (stream_out, li_output)


HALVES = 2
PLANE = 8
SIB, NEAR, FAR, ACROSS = 1, 2, 4, 8
LANES = 128
RIM = 16


def flipped(bit, flip):
    return bit + flip - 2 * bit * flip


class Place:
    def __init__(self):
        self.seat = lax.axis_index("seq")
        self.side = lax.axis_index("chan")
        self.half = self.seat // PLANE
        self.spot = lax.rem(self.seat, PLANE)
        self.bits = (lax.rem(self.spot, 2), lax.rem(self.spot // 2, 2), self.spot // 4)

    def spot_at(self, code):
        return sum(flipped(self.bits[i], (code >> i) & 1) << i for i in range(3))

    def pair_at(self, code):
        return flipped(self.bits[1], code & 1) + 2 * flipped(self.bits[2], (code >> 1) & 1)

    def half_at(self, flip):
        return flipped(self.half, flip)

    def side_at(self, code):
        return flipped(self.side, (code >> 3) & 1)

    def target(self, flip, code):
        if code == ACROSS:
            return {"chan": 1 - self.side}
        return {"seq": self.half_at(flip) * PLANE + self.spot_at(code)}


def tapped(extended, weights, start, rows):
    total = weights[0:1] * extended[start : start + rows]
    for lag in (1, 2):
        total = total + weights[lag : lag + 1] * extended[start - lag : start - lag + rows]
    return total


def added(terms):
    while len(terms) > 1:
        odd = terms[-1:] if len(terms) % 2 else []
        terms = [a + b for a, b in zip(terms[::2], terms[1::2])] + odd
    return terms[0]


def window(start, size):
    return pl.ds(pl.multiple_of(start, size), size)


SCHEDULE = {
    "open": [("mid", 1, 0, 0)],
    "gathered": [("mid", 1, 0, 1), ("mid", 1, 1, 0)],
    "spread": [("end", 1, 0, 0), ("end", 1, 1, 0), ("all", 0, 0, 0), ("all", 0, 1, 0)],
    "late": [
        ("mid", 1, 1, 1), ("end", 1, 0, 1), ("end", 1, 1, 1), ("all", 0, 0, 1), ("all", 0, 1, 1)
    ],
}


def layer_kernel(
    proj_in, stream_in, out_weights, weights, mr_short_in, base_in, li_short_in, res_in, rate_in,
    skip_in, stream_ref, out_ref,
    proj, tail, rim, mr_short, base, li_short, res, rate, skip,
    gated, cols, kept, outgoing, incoming, base_rows, block, spread, pieces,
    inverse, mixed, edge, values, openers, partial, ends, starts, state_out, state_in, turned,
    load_sem, halo_send, halo_recv, w_sem, sin_send, sin_recv, gat_send, gat_recv, x_send, x_recv,
    a_send, a_recv, b_send, b_recv, edge_sem, state_sem, out_send, out_recv,
):
    place = Place()
    spot, half, side, seat = place.spot, place.half, place.side, place.seat
    seats = lax.axis_size("seq")
    _, rows, depth = proj.shape
    part = rows // 2
    wide = cols.shape[2]
    taps = base.shape[1] // 2
    keep = tail.shape[1]
    groups = pieces.shape[0]
    chans = groups * LANES
    modes = res.shape[0]
    everyone = [(f, r) for f in (0, 1) for r in range(PLANE) if (f, r) != (0, 0)]
    started = []
    counter = iter(range(load_sem.shape[0]))

    def load(source, target):
        copy = pltpu.make_async_copy(source, target, load_sem.at[next(counter)])
        copy.start()
        return copy

    first_loads = [
        load(proj_in, proj), load(mr_short_in, mr_short), load(base_in, base),
    ]
    mine = window(side * part, part)
    late_loads = [
        load(out_weights, cols.at[0]), load(li_short_in, li_short), load(res_in, res),
        load(rate_in, rate), load(skip_in, skip),
    ]
    for f in (0, 1):
        at = window((place.half_at(f) * PLANE + spot) * wide, wide)
        late_loads.append(
            load(stream_in.at[mine, at], base_rows.at[spot, :, pl.ds(f * wide, wide)])
        )
    for g in range(groups):
        at = window(spot * chans + g * LANES, LANES)
        late_loads.append(load(weights.at[:, :, at], pieces.at[g, spot, 0]))

    barrier = pltpu.get_barrier_semaphore()
    for f, r in everyone:
        pl.semaphore_signal(barrier, inc=1, device_id=place.target(f, r))
    pl.semaphore_signal(barrier, inc=1, device_id=place.target(0, ACROSS))
    pl.semaphore_wait(barrier, len(everyone) + 1)

    def remote(source, lands, send, recv, target):
        return pltpu.make_async_remote_copy(
            src_ref=source, dst_ref=lands, send_sem=send, recv_sem=recv, device_id=target
        )

    def go(copy):
        copy.start()
        started.append(copy)

    following = {"seq": jnp.minimum(seat + 1, seats - 1)}
    halo = [
        remote(
            proj_in.at[pl.ds(1, 2), pl.ds(rows - keep, keep)], tail,
            halo_send.at[0], halo_recv.at[0], following,
        ),
        remote(
            proj_in.at[0, pl.ds(rows - RIM, RIM)], rim,
            halo_send.at[1], halo_recv.at[1], following,
        ),
    ]

    @pl.when(seat < seats - 1)
    def _():
        for copy in halo:
            copy.start()

    go(remote(out_weights, cols.at[1], w_sem.at[0], w_sem.at[1], place.target(1, 0)))
    for code in range(1, PLANE):
        for f in (0, 1):
            at = window((place.half_at(f) * PLANE + place.spot_at(code)) * wide, wide)
            go(
                remote(
                    stream_in.at[mine, at], base_rows.at[spot, :, pl.ds(f * wide, wide)],
                    sin_send.at[code * 2 + f], sin_recv.at[code * 2 + f], place.target(0, code),
                )
            )

    def base_wait(code, f):
        lands = base_rows.at[place.spot_at(code), :, pl.ds(f * wide, wide)]
        remote(
            lands, lands, sin_send.at[0], sin_recv.at[code * 2 + f], place.target(0, SIB)
        ).wait_recv()

    def piece_copy(f, code, g):
        at = window(place.spot_at(code) * chans + g * LANES, LANES)
        index = (g * 2 + f) * PLANE + code
        return remote(
            weights.at[:, :, at], pieces.at[g, spot, f], b_send.at[index], b_recv.at[index],
            place.target(f, code),
        )

    def piece_wait(f, code, g):
        lands = pieces.at[g, place.spot_at(code), f]
        index = (g * 2 + f) * PLANE + code
        remote(lands, lands, b_send.at[0], b_recv.at[index], place.target(0, SIB)).wait_recv()

    inner = flipped(half, place.bits[2])

    def release(point):
        for who, f, near, g in SCHEDULE[point]:
            codes = [r for r in range(PLANE) if (r >> 1) & 1 == near and (f, r) != (0, 0)]
            copies = [piece_copy(f, r, g) for r in codes]
            if who == "all":
                for copy in copies:
                    copy.start()
            else:

                @pl.when(inner == (1 if who == "mid" else 0))
                def _():
                    for copy in copies:
                        copy.start()

    release("open")
    for copy in first_loads:
        copy.wait()

    @pl.when(seat > 0)
    def _():
        for copy in halo:
            copy.wait_recv()

    @pl.when(seat == 0)
    def _():
        tail[...] = jnp.zeros_like(tail)
        rim[...] = jnp.zeros_like(rim)

    blocks = rows // taps
    lane = lax.broadcasted_iota(jnp.int32, (taps, blocks * LANES), 1)
    member = lax.rem(lane, LANES) // GROUP
    members = LANES // GROUP

    def mix(i, carry):
        at = window(i * LANES, LANES)
        parts = []
        for p in (1, 2):
            extended = jnp.concatenate([tail[p - 1, :, at], proj[p, :, at]], axis=0)
            parts.append(
                tapped(extended.astype(jnp.float32), mr_short[p, :, at], keep - taps, rows + taps)
            )
        value = (parts[0] * parts[1]).astype(jnp.bfloat16)
        operand = jnp.concatenate(
            [value[b * taps : b * taps + 2 * taps] for b in range(blocks)], axis=1
        )
        table = base[window(i * members, members), :]
        picked = None
        for g in range(members):
            row = jnp.broadcast_to(table[g : g + 1, :], (taps, 2 * taps))
            band = pltpu.roll(row, 0, 1, stride=1, stride_axis=0).astype(jnp.bfloat16)
            product = jnp.dot(band, operand, preferred_element_type=jnp.float32)
            picked = product if picked is None else jnp.where(member == g, product, picked)
        extended = jnp.concatenate([rim[:, at], proj[0, :, at]], axis=0).astype(jnp.float32)
        queries = tapped(extended, mr_short[0, :, at], RIM, rows)
        for b in range(blocks):
            gated[spot, pl.ds(b * taps, taps), at] = (
                queries[b * taps : (b + 1) * taps] * picked[:, b * LANES : (b + 1) * LANES]
            ).astype(gated.dtype)
        return carry

    span = depth // 2

    def gather(dim, code, s):
        lands = gated.at[place.spot_at(code), :, pl.ds(s * span, span)]
        index = {SIB: 0, NEAR: 1, FAR: 2}[dim]
        go(
            remote(
                lands, lands, gat_send.at[(index * PLANE + code) * 2 + s],
                gat_recv.at[(code ^ dim) * 2 + s], place.target(0, dim),
            )
        )

    def gathered(code, s):
        lands = gated.at[place.spot_at(code), :, pl.ds(s * span, span)]
        remote(
            lands, lands, gat_send.at[0], gat_recv.at[code * 2 + s], place.target(0, SIB)
        ).wait_recv()

    tiles = depth // LANES
    lax.fori_loop(0, tiles // 2, mix, 0)
    for dim in (NEAR, FAR, SIB):
        gather(dim, 0, 0)
    lax.fori_loop(tiles // 2, tiles, mix, 0)
    for dim in (FAR, NEAR, SIB):
        gather(dim, 0, 1)

    def pair(code):
        return pl.ds(place.pair_at(code) * 2, 2)

    def swap(k, f):
        return remote(
            outgoing.at[k, f], incoming.at[k, f], x_send.at[k * 2 + f], x_recv.at[k * 2 + f],
            place.target(0, ACROSS),
        )

    def multiply(k, f):
        for who in (1, 0):
            at = window(flipped(side, who) * part, part)
            left = gated[pair(k), at, :].reshape(2 * part, depth)
            product = jnp.dot(left, cols[f], preferred_element_type=jnp.float32)
            product = product.reshape(2, part, wide)
            if who:
                outgoing[k, f] = product.astype(outgoing.dtype)
                go(swap(k, f))
            else:
                kept[k, f] = product

    def spread_slot(code, k):
        return spread.at[
            place.spot_at(code & 7), pair(((code >> 1) & 3) ^ k), place.side_at(code)
        ]

    def scatter(dim, code, k):
        index = {SIB: 0, NEAR: 1, FAR: 2, ACROSS: 3}[dim]
        lands = spread_slot(code, k)
        go(
            remote(
                block.at[k] if code == 0 else lands, lands,
                a_send.at[(index * 16 + code) * 4 + k], a_recv.at[(code ^ dim) * 4 + k],
                place.target(0, dim),
            )
        )

    def finish(k):
        for f in (0, 1):
            swap(k, f).wait_recv()
            for code in (2 * k, 2 * k + 1):
                if code:
                    base_wait(code, f)
            at = slice(f * wide, (f + 1) * wide)
            total = (
                base_rows[pair(k), :, at].astype(jnp.float32)
                + kept[k, f]
                + incoming[k, f].astype(jnp.float32)
            )
            block[k, :, :, at] = total.astype(block.dtype)
        spread[spot, pair(k), side] = block[k]
        for dim in (ACROSS, FAR, NEAR, SIB):
            scatter(dim, 0, k)

    def onward(code, k):
        lands = spread_slot(code, k)
        remote(
            lands, lands, a_send.at[0], a_recv.at[code * 4 + k], place.target(0, SIB)
        ).wait_recv()
        if code & SIB:
            return
        order = (FAR, NEAR, ACROSS) if k != 3 else (FAR, ACROSS, NEAR)
        last = max(i for i, dim in enumerate(order) if code & dim)
        for dim in order[last + 1 :] + (SIB,):
            scatter(dim, code, k)

    for copy in late_loads:
        copy.wait()
    for s in (0, 1):
        gathered(SIB, s)
    multiply(0, 0)
    gathered(NEAR, 0)
    gather(FAR, NEAR, 0)
    gather(SIB, NEAR, 0)
    gathered(FAR, 1)
    gather(NEAR, FAR, 1)
    gather(SIB, FAR, 1)
    release("gathered")
    gathered(NEAR, 1)
    gather(SIB, NEAR, 1)
    gathered(FAR, 0)
    gather(SIB, FAR, 0)
    for s in (0, 1):
        gathered(NEAR | SIB, s)
    multiply(1, 0)
    for s in (0, 1):
        gathered(FAR | SIB, s)
    multiply(2, 0)
    remote(cols.at[1], cols.at[1], w_sem.at[0], w_sem.at[1], place.target(1, 0)).wait_recv()
    multiply(0, 1)
    multiply(1, 1)
    finish(0)
    multiply(2, 1)
    finish(1)
    for s in (0, 1):
        gathered(NEAR | FAR, s)
        gather(SIB, NEAR | FAR, s)
    onward(FAR, 0)
    finish(2)
    for s in (0, 1):
        gathered(NEAR | FAR | SIB, s)
    multiply(3, 0)
    multiply(3, 1)
    onward(FAR, 1)
    onward(NEAR, 0)
    onward(FAR, 2)
    onward(NEAR | FAR, 0)
    finish(3)
    release("spread")
    onward(NEAR, 1)
    onward(NEAR, 2)
    onward(FAR, 3)
    onward(NEAR | FAR, 1)
    onward(NEAR | FAR, 2)
    for code in (8, 12):
        onward(code, 3)
    release("late")
    for k in range(3):
        for code in (8, 12, 10, 14):
            onward(code, k)
    for code in (2, 6, 10, 14):
        onward(code, 3)
    for k in range(4):
        for code in range(1, 16, 2):
            onward(code, k)

    stream_copies = []
    at = window(flipped(half, side) * wide, wide)
    for other in range(PLANE):
        stream_copies.append(
            load(spread.at[other, spot, :, :, at], stream_ref.at[:, :, pl.ds(other * wide, wide)])
        )

    width = PLANE * HALVES * wide

    def product(slot, g):
        left = [spread[other, slot].reshape(rows, HALVES * wide) for other in range(PLANE)]
        where = window(slot * rows, rows)
        if g == 0:
            squares = None
            for piece in left:
                piece = piece.astype(jnp.float32)
                for at in range(0, HALVES * wide, LANES):
                    term = piece[:, at : at + LANES] * piece[:, at : at + LANES]
                    squares = term if squares is None else squares + term
            mean = jnp.sum(squares, axis=1, keepdims=True) / width
            inverse[where, :] = jnp.broadcast_to(lax.rsqrt(mean + EPSILON), (rows, LANES))
        scale = inverse[where, :]
        right = jnp.concatenate(
            [pieces[g, :, :, p].reshape(width, LANES) for p in range(3)], axis=1
        )
        raw = jnp.dot(jnp.concatenate(left, axis=1), right, preferred_element_type=jnp.float32)
        at = pl.ds(pl.multiple_of(RIM + slot * rows, RIM), rows)
        for p in range(3):
            scaled = raw[:, p * LANES : (p + 1) * LANES] * scale
            mixed[p, at, :] = scaled.astype(jnp.bfloat16).astype(jnp.float32)

    later = (half > 0).astype(jnp.float32)
    other_half = place.target(1, 0)

    def filtered(g):
        for f, code in everyone:
            piece_wait(f, code, g)
        product(PLANE - 1, g)
        rim_copy = remote(
            mixed.at[:, pl.ds(PLANE * rows, RIM)], edge.at[g],
            edge_sem.at[g * 2], edge_sem.at[g * 2 + 1], other_half,
        )
        rim_copy.start()

        def body(slot, carry):
            product(slot, g)
            return carry

        lax.fori_loop(0, PLANE - 1, body, 0)
        rim_copy.wait()
        mixed[:, 0:RIM, :] = edge[g] * later
        at = window(spot * chans + g * LANES, LANES)
        for slot in range(PLANE):
            here = slice(slot * rows, (slot + 1) * rows)
            terms = []
            for p in range(3):
                taps_of = li_short[p, :, at]
                start = RIM + slot * rows
                total = taps_of[0:1] * mixed[p, start : start + rows, :]
                for lag in (1, 2):
                    total = total + taps_of[lag : lag + 1] * mixed[p, start - lag : start - lag + rows, :]
                terms.append(total)
            openers[here, :] = terms[0]
            values[here, :] = (terms[1] * terms[2]).astype(jnp.bfloat16).astype(jnp.float32)

        rates = rate[:, at]
        gains = res[:, at]
        decay = jnp.exp(-rates)

        def spreaded(table, r):
            return jnp.broadcast_to(table[r : r + 1], (PLANE, LANES))

        decays = [spreaded(decay, r) for r in range(modes)]
        weighted = [spreaded(gains, r) for r in range(modes)]

        def step(t, states):
            where = pl.ds(t, PLANE, stride=rows)
            value = values[where, :]
            states = tuple(d * s + value for d, s in zip(decays, states))
            partial[where, :] = added([w * s for w, s in zip(weighted, states)])
            return states

        states = lax.fori_loop(
            0, rows, step, tuple(jnp.zeros((PLANE, LANES), jnp.float32) for _ in range(modes)),
            unroll=4,
        )
        for r in range(modes):
            ends[:, r, :] = states[r]
        leap = jnp.exp(-rates * rows)
        total = jnp.zeros((modes, LANES), jnp.float32)
        for slot in range(PLANE):
            total = leap * total + ends[slot]
        state_out[g] = total
        state_copy = remote(
            state_out.at[g], state_in.at[g], state_sem.at[g * 2], state_sem.at[g * 2 + 1], other_half
        )
        state_copy.start()
        state_copy.wait()
        total = state_in[g] * later
        opening = gains * decay
        for slot in range(PLANE):
            first = opening * total
            for r in range(modes):
                starts[r, slot : slot + 1, :] = first[r : r + 1]
            total = leap * total + ends[slot]
        direct = spreaded(skip[:, at], 0)

        def close(t, states):
            where = pl.ds(t, PLANE, stride=rows)
            total = added(list(states) + [partial[where, :], direct * values[where, :]])
            partial[where, :] = openers[where, :] * total
            return tuple(d * s for d, s in zip(decays, states))

        lax.fori_loop(0, rows, close, tuple(starts[r] for r in range(modes)), unroll=4)
        mine = window(spot * chans + g * LANES, LANES)
        for code in list(range(1, PLANE)) + [0]:
            here = window(place.spot_at(code) * rows, rows)
            turned[g, code] = partial[here, :].T.astype(turned.dtype)
            if code:
                index = g * PLANE + code
                go(
                    remote(
                        turned.at[g, code], out_ref.at[mine], out_send.at[index],
                        out_recv.at[index], place.target(0, code),
                    )
                )
            else:
                stream_copies.append(load(turned.at[g, 0], out_ref.at[mine]))

    for g in range(groups):
        filtered(g)
    for g in range(groups):
        for code in range(1, PLANE):
            lands = out_ref.at[window(place.spot_at(code) * chans + g * LANES, LANES)]
            remote(
                turned.at[g, code], lands, out_send.at[0], out_recv.at[g * PLANE + code],
                place.target(0, SIB),
            ).wait_recv()
    for copy in stream_copies:
        copy.wait()
    for copy in started:
        copy.wait_send()
    for g in range(groups):
        for f, code in everyone:
            piece_copy(f, code, g).wait_send()

    @pl.when(seat < seats - 1)
    def _():
        for copy in halo:
            copy.wait_send()


def layer(proj, stream_in, out_weights, weights, mr_short, base, li_short, res, rate, skip):
    _, rows, width = proj.shape
    part = rows // 2
    depth, wide = out_weights.shape
    deep = weights.shape[1]
    groups = width // PLANE // LANES
    taps = base.shape[1] // 2
    modes = res.shape[0]
    length = PLANE * rows
    dma = pltpu.SemaphoreType.DMA
    anywhere = pl.BlockSpec(memory_space=pl.ANY)
    bf16, f32 = jnp.bfloat16, jnp.float32
    vmem = pltpu.VMEM
    return pl.pallas_call(
        layer_kernel,
        out_shape=[
            jax.ShapeDtypeStruct((2, part, PLANE * wide), bf16),
            jax.ShapeDtypeStruct((width, rows), bf16),
        ],
        in_specs=[anywhere] * 10,
        out_specs=[anywhere] * 2,
        scratch_shapes=[
            vmem(proj.shape, bf16),
            vmem((2, taps + RIM, width), bf16),
            vmem((RIM, width), bf16),
            vmem(mr_short.shape, f32),
            vmem(base.shape, f32),
            vmem(li_short.shape, f32),
            vmem(res.shape, f32),
            vmem(rate.shape, f32),
            vmem(skip.shape, f32),
            vmem((PLANE, rows, depth), bf16),
            vmem((HALVES, depth, wide), bf16),
            vmem((4, HALVES, 2, part, wide), f32),
            vmem((4, HALVES, 2, part, wide), bf16),
            vmem((4, HALVES, 2, part, wide), bf16),
            vmem((PLANE, part, HALVES * wide), bf16),
            vmem((4, 2, part, HALVES * wide), bf16),
            vmem((PLANE, PLANE, 2, part, HALVES * wide), bf16),
            vmem((groups, PLANE, HALVES, 3, deep, LANES), bf16),
            vmem((length, LANES), f32),
            vmem((3, RIM + length, LANES), f32),
            vmem((groups, 3, RIM, LANES), f32),
            vmem((length, LANES), f32),
            vmem((length, LANES), f32),
            vmem((length, LANES), f32),
            vmem((PLANE, modes, LANES), f32),
            vmem((modes, PLANE, LANES), f32),
            vmem((groups, modes, LANES), f32),
            vmem((groups, modes, LANES), f32),
            vmem((groups, PLANE, LANES, rows), bf16),
            dma((32,)),
            dma((2,)),
            dma((2,)),
            dma((2,)),
            dma((2 * PLANE,)),
            dma((2 * PLANE,)),
            dma((3 * PLANE * 2,)),
            dma((PLANE * 2,)),
            dma((8,)),
            dma((8,)),
            dma((4 * 16 * 4,)),
            dma((16 * 4,)),
            dma((groups * 2 * PLANE,)),
            dma((groups * 2 * PLANE,)),
            dma((groups * 2,)),
            dma((groups * 2,)),
            dma((groups * PLANE,)),
            dma((groups * PLANE,)),
        ],
        compiler_params=pltpu.CompilerParams(
            collective_id=2, has_side_effects=True, vmem_limit_bytes=63 * 1024 * 1024
        ),
    )(proj, stream_in, out_weights, weights, mr_short, base, li_short, res, rate, skip)


def local_halves(
    stream_in,
    mr_proj,
    mr_short,
    mr_filter,
    mr_out,
    li_gain,
    li_in,
    li_short,
    li_res,
    li_rate,
    li_skip,
):
    row_count, _, width = mr_proj.shape
    taps = mr_filter.shape[1]
    seat = lax.axis_index("seq")
    gain = lax.dynamic_slice_in_dim(li_gain, seat * li_in.shape[0], li_in.shape[0], 0)
    weights = (jnp.transpose(li_in, (1, 0, 2)) * gain[None, :, None]).astype(jnp.bfloat16)
    base = jnp.pad(mr_filter[:, ::-1], ((0, 0), (1, taps - 1)))
    stream, filtered = layer(
        jnp.transpose(mr_proj, (1, 0, 2)), stream_in, mr_out, weights, mr_short, base, li_short,
        li_res, li_rate, li_skip[None],
    )
    return stream.reshape(row_count, width), filtered


def local(*arrays):
    halves = lax.axis_size("chan") == 2 and lax.axis_size("seq") == HALVES * PLANE
    return (local_halves if halves else local_general)(*arrays)


def solution(mesh):
    in_specs = (
        P("seq", None),
        P("seq", None, "chan"),
        P(None, None, "chan"),
        P("chan", None),
        P("chan", "seq"),
        P(),
        P("seq", None, "chan"),
        P(None, None, "chan"),
        P(None, "chan"),
        P(None, "chan"),
        P("chan"),
    )
    out_specs = (P("seq", "chan"), P("chan", "seq"))
    return jax.shard_map(local, mesh=mesh, in_specs=in_specs, out_specs=out_specs, check_vma=False)
```

```python
import functools

import jax
import jax.numpy as jnp
from jax import lax
from jax.experimental import pallas as pl
from jax.experimental.pallas import tpu as pltpu
from jax.sharding import PartitionSpec as P

GROUP = 16


EPSILON = 1e-06
HIGHEST = lax.Precision.HIGHEST


def passed_along(block, axis, distance):
    devices = range(lax.axis_size(axis))
    route = [(i - distance, i) for i in devices if i - distance in devices]
    return lax.ppermute(block, axis, route)


def band_matrices(filters):
    tap_count = filters.shape[1]
    out_index = jnp.arange(tap_count, dtype=jnp.int32)[:, None, None]
    in_index = jnp.arange(2 * tap_count, dtype=jnp.int32)[None, :, None]
    lag_index = jnp.arange(tap_count, dtype=jnp.int32)[None, None, :]
    selector = (out_index + tap_count - 1 - in_index == lag_index).astype(jnp.bfloat16)
    return jnp.einsum(
        "gj,isj->gis", filters.astype(jnp.bfloat16), selector, preferred_element_type=jnp.float32
    ).astype(jnp.bfloat16)


def lagged_rows(extended, weights, row_count):
    running = weights[:, 0][None] * extended[2 : 2 + row_count]
    for lag_index in (1, 2):
        running = (
            running
            + weights[:, lag_index][None] * extended[2 - lag_index : 2 - lag_index + row_count]
        )
    return running


def swapped(blocks, axis):
    count = lax.axis_size(axis)
    if count != 2:
        return lax.all_to_all(blocks, axis, split_axis=0, concat_axis=0, tiled=True)
    me = lax.axis_index(axis)
    mine = lax.dynamic_index_in_dim(blocks, me, 0, keepdims=False)
    other = lax.dynamic_index_in_dim(blocks, 1 - me, 0, keepdims=False)
    received = lax.ppermute(other, axis, [(0, 1), (1, 0)])
    first = me == 0
    return jnp.stack([jnp.where(first, mine, received), jnp.where(first, received, mine)])


def scattered(blocks, axis):
    count = lax.axis_size(axis)
    me = lax.axis_index(axis)
    chips, chip = count // 2, me // 2
    pairs = blocks.reshape((chips, 2) + blocks.shape[1:])
    pieces = []
    for k in range(chips):
        piece = lax.dynamic_index_in_dim(pairs, lax.rem(chip + k, chips), 0, keepdims=False)
        if k:
            route = [(i, (i + 2 * k) % count) for i in range(count)]
            piece = lax.ppermute(piece, axis, route)
        pieces.append(piece)
    return pieces


def assembled(pieces, axis):
    count = lax.axis_size(axis)
    me = lax.axis_index(axis)
    chips, chip, core = count // 2, me // 2, lax.rem(me, 2)
    kept = jnp.stack([lax.dynamic_index_in_dim(p, core, 0, keepdims=False) for p in pieces])
    given = jnp.stack([lax.dynamic_index_in_dim(p, 1 - core, 0, keepdims=False) for p in pieces])
    taken = lax.ppermute(given, axis, [(i, i ^ 1) for i in range(count)])
    both = jnp.stack(
        [jnp.where(core == 0, kept, taken), jnp.where(core == 0, taken, kept)], axis=1
    )
    both = both[::-1]
    return lax.dynamic_slice_in_dim(
        jnp.concatenate([both, both]), lax.rem(2 * chips - 1 - chip, chips), chips, 0
    )


def branch_kernel(gated_ref, weights_ref, out_ref):
    out_ref[...] = jnp.dot(gated_ref[...], weights_ref[0], preferred_element_type=jnp.float32)


def branch_product(gated, weights):
    rows, depth = gated.shape
    blocks, _, columns = weights.shape
    return pl.pallas_call(
        branch_kernel,
        out_shape=jax.ShapeDtypeStruct((rows, blocks * columns), jnp.float32),
        grid=(blocks,),
        in_specs=[
            pl.BlockSpec((rows, depth), lambda i: (0, 0)),
            pl.BlockSpec((1, depth, columns), lambda i: (i, 0, 0)),
        ],
        out_specs=pl.BlockSpec((rows, columns), lambda i: (0, i)),
        cost_estimate=pl.CostEstimate(
            flops=2 * rows * depth * blocks * columns,
            bytes_accessed=2 * blocks * depth * columns,
            transcendentals=0,
        ),
    )(gated, weights)


PARTS = 4


def ring_kernel(chips, swaps, *refs):
    inputs, outputs, sems = refs[: 1 + swaps], refs[1 + swaps : 2 + 2 * swaps], refs[2 + 2 * swaps :]
    block_ref, out_ref = inputs[0], outputs[0]
    ring_send, ring_recv, core_send, core_recv, own_sem, swap_send, swap_recv = sems
    me = lax.axis_index("seq")
    core = lax.rem(me, 2)
    chip = me // 2
    row, column = chip // 2, lax.rem(chip, 2)
    place = row + column * (chips - 1 - 2 * row)
    sibling = me + 1 - 2 * core
    rows = block_ref.shape[0] // PARTS

    def device(position, core_index):
        position = lax.rem(position + 2 * chips, chips)
        second = position // (chips // 2)
        at_row = position + second * (chips - 1 - 2 * position)
        return (2 * at_row + second) * 2 + core_index

    following, preceding = device(place + 1, core), device(place - 1, core)
    barrier = pltpu.get_barrier_semaphore()
    for target in (following, preceding, sibling):
        pl.semaphore_signal(barrier, inc=1, device_id={"seq": target})
    if swaps:
        partner = 1 - lax.axis_index("chan")
        pl.semaphore_signal(barrier, inc=1, device_id={"chan": partner})
    pl.semaphore_wait(barrier, 4 if swaps else 3)

    def ring(way, step, half, source, slot):
        part = pl.ds((2 * way + half) * rows, rows)
        index = (way * (chips - 1) + step) * 2 + half
        return pltpu.make_async_remote_copy(
            src_ref=source.at[part],
            dst_ref=out_ref.at[slot, part],
            send_sem=ring_send.at[index],
            recv_sem=ring_recv.at[index],
            device_id={"seq": (following, preceding)[way]},
        )

    def across(way, step, half, source, slot):
        part = pl.ds((2 * way + half) * rows, rows)
        index = (way * chips + step) * 2 + half
        return pltpu.make_async_remote_copy(
            src_ref=source.at[part],
            dst_ref=out_ref.at[slot, part],
            send_sem=core_send.at[index],
            recv_sem=core_recv.at[index],
            device_id={"seq": sibling},
        )

    started = []
    for step in range(chips):
        for half in (0, 1):
            for way in (0, 1):
                slot = device(place + (2 * way - 1) * step, core)
                source = block_ref if step == 0 else out_ref.at[slot]
                if step:
                    ring(way, step - 1, half, source, slot).wait_recv()
                if step < chips - 1:
                    copy = ring(way, step, half, source, slot)
                    copy.start()
                    started.append(copy)
                copy = across(way, step, half, source, slot)
                copy.start()
                started.append(copy)
        if step == 0:
            for i in range(swaps):
                copy = pltpu.make_async_remote_copy(
                    src_ref=inputs[1 + i],
                    dst_ref=outputs[1 + i],
                    send_sem=swap_send.at[i],
                    recv_sem=swap_recv.at[i],
                    device_id={"chan": partner},
                )
                copy.start()
                started.append(copy)
            own = pltpu.make_async_copy(block_ref, out_ref.at[me], own_sem)
            own.start()
    for step in range(chips):
        for half in (0, 1):
            for way in (0, 1):
                slot = device(place + (2 * way - 1) * step, 1 - core)
                across(way, step, half, out_ref.at[slot], slot).wait_recv()
    own.wait()
    for copy in started:
        copy.wait_send()
    for i in range(swaps):
        pltpu.make_async_remote_copy(
            src_ref=inputs[1 + i],
            dst_ref=outputs[1 + i],
            send_sem=swap_send.at[i],
            recv_sem=swap_recv.at[i],
            device_id={"chan": partner},
        ).wait_recv()


def gathered_rows(identity, block, *swapped_arrays):
    seq_size = lax.axis_size("seq")
    chips = seq_size // 2
    swaps = len(swapped_arrays)
    dma = pltpu.SemaphoreType.DMA
    results = pl.pallas_call(
        functools.partial(ring_kernel, chips, swaps),
        out_shape=[jax.ShapeDtypeStruct((seq_size,) + block.shape, block.dtype)]
        + [jax.ShapeDtypeStruct(a.shape, a.dtype) for a in swapped_arrays],
        in_specs=[pl.BlockSpec(memory_space=pl.ANY)] * (1 + swaps),
        out_specs=[pl.BlockSpec(memory_space=pl.ANY)] * (1 + swaps),
        scratch_shapes=[
            dma((4 * (chips - 1),)),
            dma((4 * (chips - 1),)),
            dma((4 * chips,)),
            dma((4 * chips,)),
            dma,
            dma((max(swaps, 1),)),
            dma((max(swaps, 1),)),
        ],
        compiler_params=pltpu.CompilerParams(collective_id=identity, has_side_effects=True),
    )(block, *swapped_arrays)
    return results


def summed_rows(blocks, axis):
    count = lax.axis_size(axis)
    if count != 2:
        return lax.psum_scatter(blocks.astype(jnp.bfloat16), axis, scatter_dimension=0).astype(
            jnp.float32
        )
    me = lax.axis_index(axis)
    mine = lax.dynamic_index_in_dim(blocks, me, 0, keepdims=False)
    other = lax.dynamic_index_in_dim(blocks, 1 - me, 0, keepdims=False).astype(jnp.bfloat16)
    return mine + lax.ppermute(other, axis, [(0, 1), (1, 0)]).astype(jnp.float32)


def modal_filter(values, residues, rates, skip_gain):
    chan_count, seq_length = values.shape
    size = min(128, seq_length)
    count = seq_length // size
    blocks_in = values.reshape(chan_count, count, size)
    lags = jnp.arange(size, dtype=jnp.float32)
    rising = residues[:, :, None] * jnp.exp(-rates[:, :, None] * lags)
    falling = jnp.exp(rates[:, :, None] * lags)
    product = jnp.einsum("rci,rcj->cij", rising, falling, precision=lax.Precision.HIGH)
    lower = (lags[:, None] >= lags[None, :])[None]
    matrix = jnp.where(lower, product, 0.0)
    matrix = matrix + jnp.where(
        lags[:, None] == lags[None, :], skip_gain[:, None, None], 0.0
    )
    within = jnp.einsum(
        "cij,cbj->cbi", matrix.astype(jnp.bfloat16), blocks_in, preferred_element_type=jnp.float32
    )
    ending = jnp.exp(-rates[:, :, None] * (size - 1.0 - lags)).astype(jnp.bfloat16)
    ends = jnp.einsum("rcj,cbj->rbc", ending, blocks_in, preferred_element_type=jnp.float32)
    index = jnp.arange(count, dtype=jnp.float32)
    apart = index[:, None] - 1.0 - index[None, :]
    decay = jnp.where(
        (apart >= 0.0)[None, :, :, None],
        jnp.exp(-rates[:, None, None, :] * size * jnp.maximum(apart, 0.0)[None, :, :, None]),
        0.0,
    )
    entering = jnp.sum(decay * ends[:, None], axis=2)
    rise_decay = residues[:, :, None] * jnp.exp(-rates[:, :, None] * (lags + 1.0))
    before = jnp.einsum(
        "rci,rbc->cbi",
        rise_decay.astype(jnp.bfloat16),
        entering.astype(jnp.bfloat16),
        preferred_element_type=jnp.float32,
    )
    return (within + before).reshape(chan_count, seq_length)


def lagged_time(rows, weights):
    length = rows.shape[1]
    padded = jnp.concatenate([jnp.zeros_like(rows[:, :2]), rows], axis=1).astype(jnp.float32)
    running = weights[0][:, None] * padded[:, 2:]
    for lag_index in (1, 2):
        running = running + weights[lag_index][:, None] * padded[:, 2 - lag_index : 2 - lag_index + length]
    return running


def local_general(
    stream_in,
    mr_proj,
    mr_short,
    mr_filter,
    mr_out,
    li_gain,
    li_in,
    li_short,
    li_res,
    li_rate,
    li_skip,
):
    row_count = mr_proj.shape[0]
    chan_width = mr_proj.shape[2]
    tap_count = mr_filter.shape[1]
    filter_count = mr_filter.shape[0]
    seq_size = lax.axis_size("seq")
    chan_size = lax.axis_size("chan")
    width = stream_in.shape[1]
    own_count = chan_width // seq_size
    part = row_count // chan_size
    me = lax.axis_index("chan")

    out_weights = gathered_rows(1, mr_out)[0]
    out_weights, li_in, mr_proj = lax.optimization_barrier((out_weights, li_in, mr_proj))

    in_blocks = jnp.transpose(
        li_in.reshape(li_in.shape[0], 3, seq_size, own_count), (2, 0, 1, 3)
    ).reshape(seq_size, li_in.shape[0], 3 * own_count)
    pieces = scattered(in_blocks, "seq")

    rim_rows = passed_along(mr_proj[-2:], "seq", 1)
    mr_mixed = lagged_rows(
        jnp.concatenate([rim_rows, mr_proj], axis=0).astype(jnp.float32), mr_short, row_count
    )
    queries = mr_mixed[:, 0]
    own_values = (mr_mixed[:, 1] * mr_mixed[:, 2]).astype(jnp.bfloat16)
    tail_rows = passed_along(own_values[-(tap_count - 1) :], "seq", 1)
    block_count = row_count // tap_count
    padded = jnp.concatenate(
        [tail_rows, own_values, jnp.zeros((1, chan_width), jnp.bfloat16)], axis=0
    )
    columns_major = padded.T.reshape(filter_count, GROUP, block_count + 1, tap_count)
    band_matrix = band_matrices(mr_filter)
    filtered_mr = jnp.einsum(
        "gis,gcbs->gcbi",
        band_matrix[:, :, :tap_count],
        columns_major[:, :, :-1],
        preferred_element_type=jnp.float32,
    )
    filtered_mr = filtered_mr + jnp.einsum(
        "gis,gcbs->gcbi",
        band_matrix[:, :, tap_count:],
        columns_major[:, :, 1:],
        preferred_element_type=jnp.float32,
    )
    filtered_rows = filtered_mr.reshape(chan_width, row_count).T
    gated = (queries * filtered_rows).astype(jnp.bfloat16)
    branch = branch_product(gated, out_weights)
    branch, pieces = lax.optimization_barrier((branch, pieces))
    in_own = assembled(pieces, "seq").reshape(width, 3 * own_count)
    summed = summed_rows(branch.reshape(chan_size, part, width), "chan")
    own_stream = lax.dynamic_slice_in_dim(stream_in, me * part, part, 0)
    stream = (own_stream.astype(jnp.float32) + summed).astype(jnp.bfloat16)
    stream_wide = stream.astype(jnp.float32)
    inverse_rms = lax.rsqrt(jnp.mean(stream_wide * stream_wide, axis=1, keepdims=True) + EPSILON)
    normed = (stream_wide * inverse_rms * li_gain[None]).astype(jnp.bfloat16)
    stream_parts = jnp.moveaxis(stream.reshape(part, chan_size, chan_width), 1, 0)
    if chan_size == 2:
        swap = [(0, 1), (1, 0)]
        stream_mine = lax.dynamic_index_in_dim(stream_parts, me, 0, keepdims=False)
        stream_other = lax.dynamic_index_in_dim(stream_parts, 1 - me, 0, keepdims=False)
        gathered, in_other, stream_other = gathered_rows(
            0, normed, in_own, stream_other
        )
        gathered = gathered.reshape(seq_size * part, width)
        stream_out = jnp.concatenate(
            [
                jnp.where(me == 0, stream_mine, stream_other),
                jnp.where(me == 0, stream_other, stream_mine),
            ]
        )

        def product(rows, matrix, low, high):
            return jnp.dot(
                rows,
                matrix[:, low * own_count : high * own_count],
                preferred_element_type=jnp.float32,
            ).astype(jnp.bfloat16)

        outgoing = product(gathered, in_other, 1, 3)
        sent = lax.ppermute(outgoing, "chan", swap)
        later, _ = lax.optimization_barrier((gathered, outgoing))
        outgoing_opener = product(later, in_other, 0, 1)
        sent_opener = lax.ppermute(outgoing_opener, "chan", swap)
        last, _ = lax.optimization_barrier((gathered, outgoing_opener))
        kept = product(last, in_own, 0, 3)
        kept, li_rate = lax.optimization_barrier((kept, li_rate))
        received = (sent_opener, sent[:, :own_count], sent[:, own_count:])

        def ordered(index):
            mine = kept[:, index * own_count : (index + 1) * own_count].T
            theirs = received[index].T
            pair = [
                jnp.where(me == 0, mine, theirs).reshape(own_count, seq_size, 1, part),
                jnp.where(me == 0, theirs, mine).reshape(own_count, seq_size, 1, part),
            ]
            return jnp.concatenate(pair, axis=2).reshape(own_count, seq_size * row_count)
    else:
        stream_out = swapped(stream_parts, "chan").reshape(row_count, chan_width)
        gathered = gathered_rows(0, normed)[0].reshape(seq_size * part, width)
        in_all = lax.all_gather(in_own, "chan", axis=0)
        raw = jnp.einsum(
            "xdn,td->xnt", in_all, gathered, preferred_element_type=jnp.float32
        ).astype(jnp.bfloat16)
        raw = swapped(raw, "chan").reshape(chan_size, 3, own_count, seq_size, part)
        raw = jnp.transpose(raw, (1, 2, 3, 0, 4)).reshape(3, own_count, seq_size * row_count)

        def ordered(index):
            return raw[index]

    keys, gates = ordered(1), ordered(2)
    seq_offset = lax.axis_index("seq") * own_count
    own_short = lax.dynamic_slice_in_dim(li_short, seq_offset, own_count, 2)
    own_res = lax.dynamic_slice_in_dim(li_res, seq_offset, own_count, 1)
    own_rate = lax.dynamic_slice_in_dim(li_rate, seq_offset, own_count, 1)
    own_skip = lax.dynamic_slice_in_dim(li_skip, seq_offset, own_count, 0)
    values = (lagged_time(keys, own_short[1]) * lagged_time(gates, own_short[2])).astype(
        jnp.bfloat16
    )
    filtered = modal_filter(values, own_res, own_rate, own_skip)
    if chan_size == 2:
        filtered, sent_opener = lax.optimization_barrier((filtered, sent_opener))
        received = (sent_opener,) + received[1:]
    openers = ordered(0)
    result = (lagged_time(openers, own_short[0]) * filtered).astype(jnp.bfloat16)
    li_output = lax.all_to_all(result, "seq", split_axis=1, concat_axis=0, tiled=True)
    return (stream_out, li_output)


HALVES = 2
PLANE = 8
SIB, NEAR, FAR, ACROSS = 1, 2, 4, 8
LANES = 128
RIM = 16


def flipped(bit, flip):
    return bit + flip - 2 * bit * flip


class Place:
    def __init__(self):
        self.seat = lax.axis_index("seq")
        self.side = lax.axis_index("chan")
        self.half = self.seat // PLANE
        self.spot = lax.rem(self.seat, PLANE)
        self.bits = (lax.rem(self.spot, 2), lax.rem(self.spot // 2, 2), self.spot // 4)

    def spot_at(self, code):
        return sum(flipped(self.bits[i], (code >> i) & 1) << i for i in range(3))

    def pair_at(self, code):
        return flipped(self.bits[1], code & 1) + 2 * flipped(self.bits[2], (code >> 1) & 1)

    def half_at(self, flip):
        return flipped(self.half, flip)

    def side_at(self, code):
        return flipped(self.side, (code >> 3) & 1)

    def target(self, flip, code):
        if code == ACROSS:
            return {"chan": 1 - self.side}
        return {"seq": self.half_at(flip) * PLANE + self.spot_at(code)}


def tapped(extended, weights, start, rows):
    total = weights[0:1] * extended[start : start + rows]
    for lag in (1, 2):
        total = total + weights[lag : lag + 1] * extended[start - lag : start - lag + rows]
    return total


def added(terms):
    while len(terms) > 1:
        odd = terms[-1:] if len(terms) % 2 else []
        terms = [a + b for a, b in zip(terms[::2], terms[1::2])] + odd
    return terms[0]


def window(start, size):
    return pl.ds(pl.multiple_of(start, size), size)


TURNED = ()
SAME = (0, 1, 4, 5)
CROSS = (2, 3, 6, 7)


def pieces_of(flip, group, codes):
    return [(flip, code, group) for code in codes if (flip, code) != (0, 0)]


INNER_FIRST = pieces_of(1, 0, SAME) + pieces_of(1, 1, SAME)
INNER_REST = (
    pieces_of(1, 0, CROSS) + pieces_of(0, 0, SAME + CROSS) + pieces_of(1, 1, CROSS)
    + pieces_of(0, 1, SAME + CROSS)
)
OUTER_FIRST = []
OUTER_REST = (
    pieces_of(1, 0, SAME + CROSS) + pieces_of(0, 0, SAME + CROSS) + pieces_of(1, 1, SAME + CROSS)
    + pieces_of(0, 1, SAME + CROSS)
)
PACE = 1


def layer_kernel(
    proj_in, stream_in, out_weights, weights, mr_short_in, filter_in, gain_in, li_short_in, res_in,
    rate_in, skip_in, stream_ref, out_ref,
    proj, extended_values, rim, mr_short, filters, gain, base, li_short, res, rate, skip,
    gated, cols, kept, outgoing, incoming, base_rows, block, spread, pieces,
    lent, inverse, mixed, edge, values, partial, ends, starts, state_out, state_in, turned,
    load_sem, halo_send, halo_recv, w_sem, sin_send, sin_recv, gat_send, gat_recv, x_send, x_recv,
    a_send, a_recv, b_send, b_recv, edge_sem, state_sem, out_send, out_recv,
):
    place = Place()
    spot, half, side, seat = place.spot, place.half, place.side, place.seat
    seats = lax.axis_size("seq")
    _, rows, depth = proj.shape
    part = rows // 2
    wide = cols.shape[2]
    taps = filters.shape[1]
    chans = pieces.shape[4]
    groups = chans // LANES
    modes = res.shape[0]
    everyone = [(f, r) for f in (0, 1) for r in range(PLANE) if (f, r) != (0, 0)]
    started = []
    counter = iter(range(load_sem.shape[0]))

    def load(source, target):
        copy = pltpu.make_async_copy(source, target, load_sem.at[next(counter)])
        copy.start()
        return copy

    first_loads = [
        load(proj_in, proj), load(mr_short_in, mr_short), load(filter_in, filters),
    ]
    gain_loads = [
        load(weights, lent), load(gain_in, gain),
    ]
    mine = window(side * part, part)
    late_loads = [
        load(out_weights, cols.at[0]), load(li_short_in, li_short), load(res_in, res),
        load(rate_in, rate), load(skip_in, skip),
    ]
    for f in (0, 1):
        at = window((place.half_at(f) * PLANE + spot) * wide, wide)
        late_loads.append(
            load(stream_in.at[mine, at], base_rows.at[spot, :, pl.ds(f * wide, wide)])
        )

    barrier = pltpu.get_barrier_semaphore()
    for f, r in everyone:
        pl.semaphore_signal(barrier, inc=1, device_id=place.target(f, r))
    pl.semaphore_signal(barrier, inc=1, device_id=place.target(0, ACROSS))
    pl.semaphore_wait(barrier, len(everyone) + 1)

    def remote(source, lands, send, recv, target):
        return pltpu.make_async_remote_copy(
            src_ref=source, dst_ref=lands, send_sem=send, recv_sem=recv, device_id=target
        )

    def go(copy):
        copy.start()
        started.append(copy)

    following = {"seq": jnp.minimum(seat + 1, seats - 1)}
    halo = [
        remote(
            proj_in.at[:, pl.ds(rows - RIM, RIM)], rim,
            halo_send.at[0], halo_recv.at[0], following,
        ),
        remote(
            extended_values.at[pl.ds(rows, taps)], extended_values.at[pl.ds(0, taps)],
            halo_send.at[1], halo_recv.at[1], following,
        ),
    ]

    @pl.when(seat < seats - 1)
    def _():
        halo[0].start()

    for copy in first_loads:
        copy.wait()
    tiles = depth // LANES

    def keep_values(parts, first, count, at):
        extended_values[pl.ds(taps + first, count), at] = (parts[0] * parts[1]).astype(jnp.bfloat16)

    def inner_values(i, carry):
        at = window(i * LANES, LANES)
        parts = [
            tapped(
                proj[p, taps - RIM : rows, at].astype(jnp.float32), mr_short[p, :, at], RIM, rows - taps
            )
            for p in (1, 2)
        ]
        keep_values(parts, taps, rows - taps, at)
        return carry

    def outer_values(i, carry):
        at = window(i * LANES, LANES)
        parts = [
            tapped(
                jnp.concatenate([rim[p, :, at], proj[p, 0:taps, at]], axis=0).astype(jnp.float32),
                mr_short[p, :, at], RIM, taps,
            )
            for p in (1, 2)
        ]
        keep_values(parts, 0, taps, at)
        return carry

    lax.fori_loop(0, tiles, inner_values, 0)

    @pl.when(seat < seats - 1)
    def _():
        halo[1].start()

    go(remote(out_weights, cols.at[1], w_sem.at[0], w_sem.at[1], place.target(1, 0)))
    for code in range(1, PLANE):
        for f in (0, 1):
            at = window((place.half_at(f) * PLANE + place.spot_at(code)) * wide, wide)
            go(
                remote(
                    stream_in.at[mine, at], base_rows.at[spot, :, pl.ds(f * wide, wide)],
                    sin_send.at[code * 2 + f], sin_recv.at[code * 2 + f], place.target(0, code),
                )
            )

    def base_wait(code, f):
        lands = base_rows.at[place.spot_at(code), :, pl.ds(f * wide, wide)]
        remote(
            lands, lands, sin_send.at[0], sin_recv.at[code * 2 + f], place.target(0, SIB)
        ).wait_recv()

    subset = (pl.ds(1, 2), pl.ds(0, 1))

    def piece_copy(f, code, g):
        at = window(place.spot_at(code) * chans, chans)
        index = (g * 2 + f) * PLANE + code
        return remote(
            lent.at[subset[g], :, at], pieces.at[f, spot, subset[g]], b_send.at[index],
            b_recv.at[index], place.target(f, code),
        )

    def piece_wait(f, code, g):
        lands = pieces.at[f, place.spot_at(code), subset[g]]
        index = (g * 2 + f) * PLANE + code
        remote(lands, lands, b_send.at[0], b_recv.at[index], place.target(0, SIB)).wait_recv()

    inner = flipped(half, place.bits[2])

    def issue(inner_pieces, outer_pieces):
        for wanted, some in ((1, inner_pieces), (0, outer_pieces)):
            if some:

                @pl.when(inner == wanted)
                def _():
                    for piece in some:
                        piece_copy(*piece).start()

    queues = [list(INNER_REST), list(OUTER_REST)]

    def drip(count=PACE):
        taken = [queue[:count] for queue in queues]
        for queue in queues:
            del queue[:count]
        issue(*taken)

    for copy in gain_loads:
        copy.wait()
    deep = lent.shape[1]
    row = jnp.broadcast_to(gain[:, window(seat * deep, deep)], (PLANE, deep))
    column = jnp.broadcast_to(row.T[:, 0:1], (deep, LANES))

    def lend(i, carry):
        at = window(i * LANES, LANES)
        for p in range(3):
            lent[p, :, at] = (lent[p, :, at].astype(jnp.float32) * column).astype(lent.dtype)
        return carry

    lax.fori_loop(0, depth // LANES, lend, 0)
    late_loads.append(load(lent.at[:, :, window(spot * chans, chans)], pieces.at[0, spot]))
    issue(INNER_FIRST, OUTER_FIRST)
    source = lax.broadcasted_iota(jnp.int32, (taps, 2 * taps), 0)
    landing = lax.broadcasted_iota(jnp.int32, (taps, 2 * taps), 1)
    mirror = (source + landing == taps).astype(jnp.bfloat16)
    base[...] = jnp.dot(
        filters[...].astype(jnp.bfloat16), mirror, preferred_element_type=jnp.float32
    )

    @pl.when(seat > 0)
    def _():
        halo[0].wait_recv()

    @pl.when(seat == 0)
    def _():
        rim[...] = jnp.zeros_like(rim)
        extended_values[0:taps, :] = jnp.zeros((taps, depth), extended_values.dtype)

    lax.fori_loop(0, tiles, outer_values, 0)

    @pl.when(seat > 0)
    def _():
        halo[1].wait_recv()

    blocks = rows // taps
    lane = lax.broadcasted_iota(jnp.int32, (taps, blocks * LANES), 1)
    member = lax.rem(lane, LANES) // GROUP
    members = LANES // GROUP

    def mix(i, carry):
        at = window(i * LANES, LANES)
        operand = jnp.concatenate(
            [extended_values[b * taps : b * taps + 2 * taps, at] for b in range(blocks)], axis=1
        )
        table = base[window(i * members, members), :]
        picked = None
        for g in range(members):
            row = jnp.broadcast_to(table[g : g + 1, :], (taps, 2 * taps))
            band = pltpu.roll(row, 0, 1, stride=1, stride_axis=0).astype(jnp.bfloat16)
            product = jnp.dot(band, operand, preferred_element_type=jnp.float32)
            picked = product if picked is None else jnp.where(member == g, product, picked)
        extended = jnp.concatenate([rim[0, :, at], proj[0, :, at]], axis=0).astype(jnp.float32)
        queries = tapped(extended, mr_short[0, :, at], RIM, rows)
        for b in range(blocks):
            gated[spot, pl.ds(b * taps, taps), at] = (
                queries[b * taps : (b + 1) * taps] * picked[:, b * LANES : (b + 1) * LANES]
            ).astype(gated.dtype)
        return carry

    span = depth // 2

    def gather(dim, code, s):
        lands = gated.at[place.spot_at(code), :, pl.ds(s * span, span)]
        index = {SIB: 0, NEAR: 1, FAR: 2}[dim]
        go(
            remote(
                lands, lands, gat_send.at[(index * PLANE + code) * 2 + s],
                gat_recv.at[(code ^ dim) * 2 + s], place.target(0, dim),
            )
        )

    def gathered(code, s):
        lands = gated.at[place.spot_at(code), :, pl.ds(s * span, span)]
        remote(
            lands, lands, gat_send.at[0], gat_recv.at[code * 2 + s], place.target(0, SIB)
        ).wait_recv()

    lax.fori_loop(0, tiles // 2, mix, 0)
    for dim in (NEAR, FAR, SIB):
        gather(dim, 0, 0)
    lax.fori_loop(tiles // 2, tiles, mix, 0)
    for dim in (FAR, NEAR, SIB):
        gather(dim, 0, 1)

    def pair(code):
        return pl.ds(place.pair_at(code) * 2, 2)

    def swap(k, f):
        return remote(
            outgoing.at[k, f], incoming.at[k, f], x_send.at[k * 2 + f], x_recv.at[k * 2 + f],
            place.target(0, ACROSS),
        )

    def multiply(k, f):
        for who in (1, 0):
            at = window(flipped(side, who) * part, part)
            left = gated[pair(k), at, :].reshape(2 * part, depth)
            product = jnp.dot(left, cols[f], preferred_element_type=jnp.float32)
            product = product.reshape(2, part, wide)
            if who:
                outgoing[k, f] = product.astype(outgoing.dtype)
                go(swap(k, f))
            else:
                kept[k, f] = product

    a_counter = iter(range(a_send.shape[0]))
    a_started = []

    def spread_slot(code, k, f):
        return spread.at[
            f, place.spot_at(code & 7), pair(((code >> 1) & 3) ^ k), place.side_at(code)
        ]

    def scatter(dim, code, k, f):
        lands = spread_slot(code, k, f)
        copy = remote(
            block.at[k, f] if code == 0 else lands, lands,
            a_send.at[next(a_counter)], a_recv.at[((code ^ dim) * 4 + k) * 2 + f],
            place.target(0, dim),
        )
        copy.start()
        a_started.append(copy)

    def finish(k, f):
        swap(k, f).wait_recv()
        for code in (2 * k, 2 * k + 1):
            if code:
                base_wait(code, f)
        total = (
            base_rows[pair(k), :, f * wide : (f + 1) * wide].astype(jnp.float32)
            + kept[k, f]
            + incoming[k, f].astype(jnp.float32)
        )
        block[k, f] = total.astype(block.dtype)
        spread[f, spot, pair(k), side] = block[k, f]
        for dim in (ACROSS, FAR, NEAR, SIB):
            scatter(dim, 0, k, f)

    def onward(code, k, f):
        lands = spread_slot(code, k, f)
        remote(
            lands, lands, a_send.at[0], a_recv.at[(code * 4 + k) * 2 + f], place.target(0, SIB)
        ).wait_recv()
        if code & SIB:
            return
        order = (FAR, NEAR, ACROSS) if (k, f) not in TURNED else (FAR, ACROSS, NEAR)
        last = max(i for i, dim in enumerate(order) if code & dim)
        for dim in order[last + 1 :] + (SIB,):
            scatter(dim, code, k, f)
        if last < 2:
            drip()

    def both(action, *codes):
        for s in (0, 1):
            for code in codes:
                action(code, s)

    for copy in late_loads:
        copy.wait()
    both(gathered, SIB)
    multiply(0, 0)
    gathered(NEAR, 0)
    gather(FAR, NEAR, 0)
    gather(SIB, NEAR, 0)
    gathered(FAR, 1)
    gather(NEAR, FAR, 1)
    gather(SIB, FAR, 1)
    drip()
    finish(0, 0)
    gathered(NEAR, 1)
    gather(SIB, NEAR, 1)
    gathered(FAR, 0)
    gather(SIB, FAR, 0)
    drip()
    both(gathered, NEAR | SIB)
    drip()
    multiply(1, 0)
    both(gathered, FAR | SIB)
    drip()
    multiply(2, 0)
    finish(1, 0)
    onward(FAR, 0, 0)
    for s in (0, 1):
        gathered(NEAR | FAR, s)
        gather(SIB, NEAR | FAR, s)
    finish(2, 0)
    drip()
    both(gathered, NEAR | FAR | SIB)
    drip()
    multiply(3, 0)
    onward(NEAR, 0, 0)
    onward(FAR, 1, 0)
    onward(FAR, 2, 0)
    onward(NEAR | FAR, 0, 0)
    finish(3, 0)
    drip()
    remote(cols.at[1], cols.at[1], w_sem.at[0], w_sem.at[1], place.target(1, 0)).wait_recv()
    multiply(0, 1)
    multiply(1, 1)
    finish(0, 1)
    multiply(2, 1)
    finish(1, 1)
    multiply(3, 1)
    finish(2, 1)
    finish(3, 1)
    drip()
    onward(NEAR, 1, 0)
    onward(NEAR, 2, 0)
    for f in (0, 1):
        for k in range(4):
            for code in (FAR, NEAR, ACROSS, NEAR | FAR, ACROSS | FAR):
                done = (FAR, 0, 0), (NEAR, 0, 0), (FAR, 1, 0), (FAR, 2, 0), (NEAR | FAR, 0, 0)
                done += (NEAR, 1, 0), (NEAR, 2, 0)
                pivot = ACROSS if (k, f) in TURNED else NEAR
                if (code, k, f) not in done and (code == FAR or code & pivot):
                    onward(code, k, f)
    drip(2 * len(INNER_REST))
    for f in (0, 1):
        for k in range(4):
            pivot = NEAR if (k, f) in TURNED else ACROSS
            for code in range(2, 16, 2):
                if code & pivot:
                    onward(code, k, f)
    for f in (0, 1):
        for k in range(4):
            for code in range(1, 16, 2):
                onward(code, k, f)

    stream_copies = []
    for other in range(PLANE):
        stream_copies.append(
            load(
                spread.at[flipped(half, side), other, spot],
                stream_ref.at[:, :, pl.ds(other * wide, wide)],
            )
        )

    width = PLANE * HALVES * wide

    couples = PLANE // 2
    double = 2 * rows

    def product(couple, g):
        left = [
            spread[f, other, pl.ds(2 * couple, 2)].reshape(double, wide)
            for f in range(HALVES)
            for other in range(PLANE)
        ]
        where = window(couple * double, double)
        if g == 0:
            squares = None
            for piece in left:
                piece = piece.astype(jnp.float32)
                for at in range(0, wide, LANES):
                    term = piece[:, at : at + LANES] * piece[:, at : at + LANES]
                    squares = term if squares is None else squares + term
            mean = jnp.sum(squares, axis=1, keepdims=True) / width
            inverse[where, :] = jnp.broadcast_to(lax.rsqrt(mean + EPSILON), (double, LANES))
        scale = inverse[where, :]
        left = jnp.concatenate(left, axis=1)
        at = pl.ds(pl.multiple_of(RIM + couple * double, RIM), double)
        for slot, p in enumerate((1, 2) if g == 0 else (0,)):
            right = pieces[:, :, p].reshape(width, chans)
            raw = jnp.dot(left, right, preferred_element_type=jnp.float32)
            for c in range(groups):
                lanes = slice(c * LANES, (c + 1) * LANES)
                mixed[slot, at, lanes] = (
                    (raw[:, lanes] * scale).astype(jnp.bfloat16).astype(jnp.float32)
                )

    later = (half > 0).astype(jnp.float32)
    other_half = place.target(1, 0)
    my_chans = window(spot * chans, chans)

    def projected(g):
        for f, code in everyone:
            piece_wait(f, code, g)
        count = 2 - g
        lax.fori_loop(couples - 1, couples, lambda i, c: (product(i, g), c)[1], 0)
        rim_copy = remote(
            mixed.at[pl.ds(0, count), pl.ds(PLANE * rows, RIM)], edge.at[pl.ds(2 * g, count)],
            edge_sem.at[g * 2], edge_sem.at[g * 2 + 1], other_half,
        )
        rim_copy.start()
        lax.fori_loop(0, couples - 1, lambda i, c: (product(i, g), c)[1], 0)
        rim_copy.wait()
        mixed[0:count, 0:RIM, :] = edge[2 * g : 2 * g + count] * later

    def short_filtered(slot_index, p, slot):
        weights_of = li_short[p, :, my_chans]
        start = RIM + slot * rows
        total = weights_of[0:1] * mixed[slot_index, start : start + rows, :]
        for lag in (1, 2):
            total = total + weights_of[lag : lag + 1] * mixed[
                slot_index, start - lag : start - lag + rows, :
            ]
        return total

    def lane_group(c):
        return slice(c * LANES, (c + 1) * LANES)

    projected(0)
    for slot in range(PLANE):
        value = short_filtered(0, 1, slot) * short_filtered(1, 2, slot)
        value = value.astype(jnp.bfloat16).astype(jnp.float32)
        for c in range(groups):
            values[c, slot * rows : (slot + 1) * rows, :] = value[:, lane_group(c)]

    def spreaded(table, r):
        return jnp.broadcast_to(table[r : r + 1], (PLANE, LANES))

    rates = rate[:, my_chans]
    gains = res[:, my_chans]
    decay = jnp.exp(-rates)
    leap = jnp.exp(-rates * rows)
    for c in range(groups):
        decays = [spreaded(decay[:, lane_group(c)], r) for r in range(modes)]
        weighted = [spreaded(gains[:, lane_group(c)], r) for r in range(modes)]

        def step(t, states):
            where = pl.ds(t, PLANE, stride=rows)
            value = values[c, where, :]
            states = tuple(d * s + value for d, s in zip(decays, states))
            partial[c, where, :] = added([w * s for w, s in zip(weighted, states)])
            return states

        states = lax.fori_loop(
            0, rows, step, tuple(jnp.zeros((PLANE, LANES), jnp.float32) for _ in range(modes)),
            unroll=4,
        )
        for r in range(modes):
            ends[:, r, lane_group(c)] = states[r]
    total = jnp.zeros((modes, chans), jnp.float32)
    for slot in range(PLANE):
        total = leap * total + ends[slot]
    state_out[...] = total
    state_copy = remote(state_out, state_in, state_sem.at[0], state_sem.at[1], other_half)
    state_copy.start()
    state_copy.wait()
    total = state_in[...] * later
    opening = gains * decay
    for slot in range(PLANE):
        first = opening * total
        for r in range(modes):
            starts[r, slot : slot + 1, :] = first[r : r + 1]
        total = leap * total + ends[slot]
    for c in range(groups):
        decays = [spreaded(decay[:, lane_group(c)], r) for r in range(modes)]
        direct = spreaded(skip[:, my_chans][:, lane_group(c)], 0)

        def close(t, states):
            where = pl.ds(t, PLANE, stride=rows)
            partial[c, where, :] = added(
                list(states) + [partial[c, where, :], direct * values[c, where, :]]
            )
            return tuple(d * s for d, s in zip(decays, states))

        lax.fori_loop(
            0, rows, close, tuple(starts[r, :, lane_group(c)] for r in range(modes)), unroll=4
        )

    projected(1)
    for slot in range(PLANE):
        opener = short_filtered(0, 0, slot)
        for c in range(groups):
            gated_rows = opener[:, lane_group(c)] * partial[c, slot * rows : (slot + 1) * rows, :]
            turned[slot, c * LANES : (c + 1) * LANES, :] = gated_rows.T.astype(turned.dtype)
    for code in range(1, PLANE):
        go(
            remote(
                turned.at[place.spot_at(code)], out_ref.at[my_chans], out_send.at[code],
                out_recv.at[code], place.target(0, code),
            )
        )
    stream_copies.append(load(turned.at[spot], out_ref.at[my_chans]))
    for code in range(1, PLANE):
        lands = out_ref.at[window(place.spot_at(code) * chans, chans)]
        remote(
            turned.at[0], lands, out_send.at[0], out_recv.at[code], place.target(0, SIB)
        ).wait_recv()
    for copy in stream_copies:
        copy.wait()
    for copy in started + a_started:
        copy.wait_send()
    for g in (0, 1):
        for f, code in everyone:
            piece_copy(f, code, g).wait_send()

    @pl.when(seat < seats - 1)
    def _():
        for copy in halo:
            copy.wait_send()


def layer(proj, stream_in, out_weights, weights, mr_short, filters, gain, li_short, res, rate, skip):
    _, rows, width = proj.shape
    part = rows // 2
    depth, wide = out_weights.shape
    deep = weights.shape[1]
    chans = width // PLANE
    groups = chans // LANES
    taps = filters.shape[1]
    modes = res.shape[0]
    length = PLANE * rows
    dma = pltpu.SemaphoreType.DMA
    anywhere = pl.BlockSpec(memory_space=pl.ANY)
    bf16, f32 = jnp.bfloat16, jnp.float32
    vmem = pltpu.VMEM
    return pl.pallas_call(
        layer_kernel,
        out_shape=[
            jax.ShapeDtypeStruct((2, part, PLANE * wide), bf16),
            jax.ShapeDtypeStruct((width, rows), bf16),
        ],
        in_specs=[anywhere] * 11,
        out_specs=[anywhere] * 2,
        scratch_shapes=[
            vmem(proj.shape, bf16),
            vmem((taps + rows, width), bf16),
            vmem((3, RIM, width), bf16),
            vmem(mr_short.shape, f32),
            vmem(filters.shape, f32),
            vmem(gain.shape, f32),
            vmem((filters.shape[0], 2 * taps), f32),
            vmem(li_short.shape, f32),
            vmem(res.shape, f32),
            vmem(rate.shape, f32),
            vmem(skip.shape, f32),
            vmem((PLANE, rows, depth), bf16),
            vmem((HALVES, depth, wide), bf16),
            vmem((4, HALVES, 2, part, wide), f32),
            vmem((4, HALVES, 2, part, wide), bf16),
            vmem((4, HALVES, 2, part, wide), bf16),
            vmem((PLANE, part, HALVES * wide), bf16),
            vmem((4, HALVES, 2, part, wide), bf16),
            vmem((HALVES, PLANE, PLANE, 2, part, wide), bf16),
            vmem((HALVES, PLANE, 3, deep, chans), bf16),
            vmem(weights.shape, bf16),
            vmem((length, LANES), f32),
            vmem((2, RIM + length, chans), f32),
            vmem((3, RIM, chans), f32),
            vmem((groups, length, LANES), f32),
            vmem((groups, length, LANES), f32),
            vmem((PLANE, modes, chans), f32),
            vmem((modes, PLANE, chans), f32),
            vmem((modes, chans), f32),
            vmem((modes, chans), f32),
            vmem((PLANE, chans, rows), bf16),
            dma((32,)),
            dma((2,)),
            dma((2,)),
            dma((2,)),
            dma((2 * PLANE,)),
            dma((2 * PLANE,)),
            dma((3 * PLANE * 2,)),
            dma((PLANE * 2,)),
            dma((8,)),
            dma((8,)),
            dma((15 * 4 * HALVES,)),
            dma((16 * 4 * HALVES,)),
            dma((4 * PLANE,)),
            dma((4 * PLANE,)),
            dma((4,)),
            dma((2,)),
            dma((PLANE,)),
            dma((PLANE,)),
        ],
        compiler_params=pltpu.CompilerParams(
            collective_id=2, has_side_effects=True, vmem_limit_bytes=63 * 1024 * 1024
        ),
    )(proj, stream_in, out_weights, weights, mr_short, filters, gain, li_short, res, rate, skip)


def local_halves(
    stream_in,
    mr_proj,
    mr_short,
    mr_filter,
    mr_out,
    li_gain,
    li_in,
    li_short,
    li_res,
    li_rate,
    li_skip,
):
    row_count, _, width = mr_proj.shape
    stream, filtered = layer(
        jnp.transpose(mr_proj, (1, 0, 2)), stream_in, mr_out, jnp.transpose(li_in, (1, 0, 2)),
        mr_short, mr_filter, li_gain[None], li_short, li_res, li_rate, li_skip[None],
    )
    return stream.reshape(row_count, width), filtered


def local(*arrays):
    halves = lax.axis_size("chan") == 2 and lax.axis_size("seq") == HALVES * PLANE
    halves = halves and arrays[1].shape[0] >= 2 * arrays[3].shape[1]
    return (local_halves if halves else local_general)(*arrays)


def solution(mesh):
    in_specs = (
        P("seq", None),
        P("seq", None, "chan"),
        P(None, None, "chan"),
        P("chan", None),
        P("chan", "seq"),
        P(),
        P("seq", None, "chan"),
        P(None, None, "chan"),
        P(None, "chan"),
        P(None, "chan"),
        P("chan"),
    )
    out_specs = (P("seq", "chan"), P("chan", "seq"))
    return jax.shard_map(local, mesh=mesh, in_specs=in_specs, out_specs=out_specs, check_vma=False)
```

```python
import functools

import jax
import jax.numpy as jnp
from jax import lax
from jax.experimental import pallas as pl
from jax.experimental.pallas import tpu as pltpu
from jax.sharding import PartitionSpec as P

GROUP = 16


EPSILON = 1e-06
HIGHEST = lax.Precision.HIGHEST


def passed_along(block, axis, distance):
    devices = range(lax.axis_size(axis))
    route = [(i - distance, i) for i in devices if i - distance in devices]
    return lax.ppermute(block, axis, route)


def band_matrices(filters):
    tap_count = filters.shape[1]
    out_index = jnp.arange(tap_count, dtype=jnp.int32)[:, None, None]
    in_index = jnp.arange(2 * tap_count, dtype=jnp.int32)[None, :, None]
    lag_index = jnp.arange(tap_count, dtype=jnp.int32)[None, None, :]
    selector = (out_index + tap_count - 1 - in_index == lag_index).astype(jnp.bfloat16)
    return jnp.einsum(
        "gj,isj->gis", filters.astype(jnp.bfloat16), selector, preferred_element_type=jnp.float32
    ).astype(jnp.bfloat16)


def lagged_rows(extended, weights, row_count):
    running = weights[:, 0][None] * extended[2 : 2 + row_count]
    for lag_index in (1, 2):
        running = (
            running
            + weights[:, lag_index][None] * extended[2 - lag_index : 2 - lag_index + row_count]
        )
    return running


def swapped(blocks, axis):
    count = lax.axis_size(axis)
    if count != 2:
        return lax.all_to_all(blocks, axis, split_axis=0, concat_axis=0, tiled=True)
    me = lax.axis_index(axis)
    mine = lax.dynamic_index_in_dim(blocks, me, 0, keepdims=False)
    other = lax.dynamic_index_in_dim(blocks, 1 - me, 0, keepdims=False)
    received = lax.ppermute(other, axis, [(0, 1), (1, 0)])
    first = me == 0
    return jnp.stack([jnp.where(first, mine, received), jnp.where(first, received, mine)])


def scattered(blocks, axis):
    count = lax.axis_size(axis)
    me = lax.axis_index(axis)
    chips, chip = count // 2, me // 2
    pairs = blocks.reshape((chips, 2) + blocks.shape[1:])
    pieces = []
    for k in range(chips):
        piece = lax.dynamic_index_in_dim(pairs, lax.rem(chip + k, chips), 0, keepdims=False)
        if k:
            route = [(i, (i + 2 * k) % count) for i in range(count)]
            piece = lax.ppermute(piece, axis, route)
        pieces.append(piece)
    return pieces


def assembled(pieces, axis):
    count = lax.axis_size(axis)
    me = lax.axis_index(axis)
    chips, chip, core = count // 2, me // 2, lax.rem(me, 2)
    kept = jnp.stack([lax.dynamic_index_in_dim(p, core, 0, keepdims=False) for p in pieces])
    given = jnp.stack([lax.dynamic_index_in_dim(p, 1 - core, 0, keepdims=False) for p in pieces])
    taken = lax.ppermute(given, axis, [(i, i ^ 1) for i in range(count)])
    both = jnp.stack(
        [jnp.where(core == 0, kept, taken), jnp.where(core == 0, taken, kept)], axis=1
    )
    both = both[::-1]
    return lax.dynamic_slice_in_dim(
        jnp.concatenate([both, both]), lax.rem(2 * chips - 1 - chip, chips), chips, 0
    )


def branch_kernel(gated_ref, weights_ref, out_ref):
    out_ref[...] = jnp.dot(gated_ref[...], weights_ref[0], preferred_element_type=jnp.float32)


def branch_product(gated, weights):
    rows, depth = gated.shape
    blocks, _, columns = weights.shape
    return pl.pallas_call(
        branch_kernel,
        out_shape=jax.ShapeDtypeStruct((rows, blocks * columns), jnp.float32),
        grid=(blocks,),
        in_specs=[
            pl.BlockSpec((rows, depth), lambda i: (0, 0)),
            pl.BlockSpec((1, depth, columns), lambda i: (i, 0, 0)),
        ],
        out_specs=pl.BlockSpec((rows, columns), lambda i: (0, i)),
        cost_estimate=pl.CostEstimate(
            flops=2 * rows * depth * blocks * columns,
            bytes_accessed=2 * blocks * depth * columns,
            transcendentals=0,
        ),
    )(gated, weights)


PARTS = 4


def ring_kernel(chips, swaps, *refs):
    inputs, outputs, sems = refs[: 1 + swaps], refs[1 + swaps : 2 + 2 * swaps], refs[2 + 2 * swaps :]
    block_ref, out_ref = inputs[0], outputs[0]
    ring_send, ring_recv, core_send, core_recv, own_sem, swap_send, swap_recv = sems
    me = lax.axis_index("seq")
    core = lax.rem(me, 2)
    chip = me // 2
    row, column = chip // 2, lax.rem(chip, 2)
    place = row + column * (chips - 1 - 2 * row)
    sibling = me + 1 - 2 * core
    rows = block_ref.shape[0] // PARTS

    def device(position, core_index):
        position = lax.rem(position + 2 * chips, chips)
        second = position // (chips // 2)
        at_row = position + second * (chips - 1 - 2 * position)
        return (2 * at_row + second) * 2 + core_index

    following, preceding = device(place + 1, core), device(place - 1, core)
    barrier = pltpu.get_barrier_semaphore()
    for target in (following, preceding, sibling):
        pl.semaphore_signal(barrier, inc=1, device_id={"seq": target})
    if swaps:
        partner = 1 - lax.axis_index("chan")
        pl.semaphore_signal(barrier, inc=1, device_id={"chan": partner})
    pl.semaphore_wait(barrier, 4 if swaps else 3)

    def ring(way, step, half, source, slot):
        part = pl.ds((2 * way + half) * rows, rows)
        index = (way * (chips - 1) + step) * 2 + half
        return pltpu.make_async_remote_copy(
            src_ref=source.at[part],
            dst_ref=out_ref.at[slot, part],
            send_sem=ring_send.at[index],
            recv_sem=ring_recv.at[index],
            device_id={"seq": (following, preceding)[way]},
        )

    def across(way, step, half, source, slot):
        part = pl.ds((2 * way + half) * rows, rows)
        index = (way * chips + step) * 2 + half
        return pltpu.make_async_remote_copy(
            src_ref=source.at[part],
            dst_ref=out_ref.at[slot, part],
            send_sem=core_send.at[index],
            recv_sem=core_recv.at[index],
            device_id={"seq": sibling},
        )

    started = []
    for step in range(chips):
        for half in (0, 1):
            for way in (0, 1):
                slot = device(place + (2 * way - 1) * step, core)
                source = block_ref if step == 0 else out_ref.at[slot]
                if step:
                    ring(way, step - 1, half, source, slot).wait_recv()
                if step < chips - 1:
                    copy = ring(way, step, half, source, slot)
                    copy.start()
                    started.append(copy)
                copy = across(way, step, half, source, slot)
                copy.start()
                started.append(copy)
        if step == 0:
            for i in range(swaps):
                copy = pltpu.make_async_remote_copy(
                    src_ref=inputs[1 + i],
                    dst_ref=outputs[1 + i],
                    send_sem=swap_send.at[i],
                    recv_sem=swap_recv.at[i],
                    device_id={"chan": partner},
                )
                copy.start()
                started.append(copy)
            own = pltpu.make_async_copy(block_ref, out_ref.at[me], own_sem)
            own.start()
    for step in range(chips):
        for half in (0, 1):
            for way in (0, 1):
                slot = device(place + (2 * way - 1) * step, 1 - core)
                across(way, step, half, out_ref.at[slot], slot).wait_recv()
    own.wait()
    for copy in started:
        copy.wait_send()
    for i in range(swaps):
        pltpu.make_async_remote_copy(
            src_ref=inputs[1 + i],
            dst_ref=outputs[1 + i],
            send_sem=swap_send.at[i],
            recv_sem=swap_recv.at[i],
            device_id={"chan": partner},
        ).wait_recv()


def gathered_rows(identity, block, *swapped_arrays):
    seq_size = lax.axis_size("seq")
    chips = seq_size // 2
    swaps = len(swapped_arrays)
    dma = pltpu.SemaphoreType.DMA
    results = pl.pallas_call(
        functools.partial(ring_kernel, chips, swaps),
        out_shape=[jax.ShapeDtypeStruct((seq_size,) + block.shape, block.dtype)]
        + [jax.ShapeDtypeStruct(a.shape, a.dtype) for a in swapped_arrays],
        in_specs=[pl.BlockSpec(memory_space=pl.ANY)] * (1 + swaps),
        out_specs=[pl.BlockSpec(memory_space=pl.ANY)] * (1 + swaps),
        scratch_shapes=[
            dma((4 * (chips - 1),)),
            dma((4 * (chips - 1),)),
            dma((4 * chips,)),
            dma((4 * chips,)),
            dma,
            dma((max(swaps, 1),)),
            dma((max(swaps, 1),)),
        ],
        compiler_params=pltpu.CompilerParams(collective_id=identity, has_side_effects=True),
    )(block, *swapped_arrays)
    return results


def summed_rows(blocks, axis):
    count = lax.axis_size(axis)
    if count != 2:
        return lax.psum_scatter(blocks.astype(jnp.bfloat16), axis, scatter_dimension=0).astype(
            jnp.float32
        )
    me = lax.axis_index(axis)
    mine = lax.dynamic_index_in_dim(blocks, me, 0, keepdims=False)
    other = lax.dynamic_index_in_dim(blocks, 1 - me, 0, keepdims=False).astype(jnp.bfloat16)
    return mine + lax.ppermute(other, axis, [(0, 1), (1, 0)]).astype(jnp.float32)


def modal_filter(values, residues, rates, skip_gain):
    chan_count, seq_length = values.shape
    size = min(128, seq_length)
    count = seq_length // size
    blocks_in = values.reshape(chan_count, count, size)
    lags = jnp.arange(size, dtype=jnp.float32)
    rising = residues[:, :, None] * jnp.exp(-rates[:, :, None] * lags)
    falling = jnp.exp(rates[:, :, None] * lags)
    product = jnp.einsum("rci,rcj->cij", rising, falling, precision=lax.Precision.HIGH)
    lower = (lags[:, None] >= lags[None, :])[None]
    matrix = jnp.where(lower, product, 0.0)
    matrix = matrix + jnp.where(
        lags[:, None] == lags[None, :], skip_gain[:, None, None], 0.0
    )
    within = jnp.einsum(
        "cij,cbj->cbi", matrix.astype(jnp.bfloat16), blocks_in, preferred_element_type=jnp.float32
    )
    ending = jnp.exp(-rates[:, :, None] * (size - 1.0 - lags)).astype(jnp.bfloat16)
    ends = jnp.einsum("rcj,cbj->rbc", ending, blocks_in, preferred_element_type=jnp.float32)
    index = jnp.arange(count, dtype=jnp.float32)
    apart = index[:, None] - 1.0 - index[None, :]
    decay = jnp.where(
        (apart >= 0.0)[None, :, :, None],
        jnp.exp(-rates[:, None, None, :] * size * jnp.maximum(apart, 0.0)[None, :, :, None]),
        0.0,
    )
    entering = jnp.sum(decay * ends[:, None], axis=2)
    rise_decay = residues[:, :, None] * jnp.exp(-rates[:, :, None] * (lags + 1.0))
    before = jnp.einsum(
        "rci,rbc->cbi",
        rise_decay.astype(jnp.bfloat16),
        entering.astype(jnp.bfloat16),
        preferred_element_type=jnp.float32,
    )
    return (within + before).reshape(chan_count, seq_length)


def lagged_time(rows, weights):
    length = rows.shape[1]
    padded = jnp.concatenate([jnp.zeros_like(rows[:, :2]), rows], axis=1).astype(jnp.float32)
    running = weights[0][:, None] * padded[:, 2:]
    for lag_index in (1, 2):
        running = running + weights[lag_index][:, None] * padded[:, 2 - lag_index : 2 - lag_index + length]
    return running


def local_general(
    stream_in,
    mr_proj,
    mr_short,
    mr_filter,
    mr_out,
    li_gain,
    li_in,
    li_short,
    li_res,
    li_rate,
    li_skip,
):
    row_count = mr_proj.shape[0]
    chan_width = mr_proj.shape[2]
    tap_count = mr_filter.shape[1]
    filter_count = mr_filter.shape[0]
    seq_size = lax.axis_size("seq")
    chan_size = lax.axis_size("chan")
    width = stream_in.shape[1]
    own_count = chan_width // seq_size
    part = row_count // chan_size
    me = lax.axis_index("chan")

    out_weights = gathered_rows(1, mr_out)[0]
    out_weights, li_in, mr_proj = lax.optimization_barrier((out_weights, li_in, mr_proj))

    in_blocks = jnp.transpose(
        li_in.reshape(li_in.shape[0], 3, seq_size, own_count), (2, 0, 1, 3)
    ).reshape(seq_size, li_in.shape[0], 3 * own_count)
    pieces = scattered(in_blocks, "seq")

    rim_rows = passed_along(mr_proj[-2:], "seq", 1)
    mr_mixed = lagged_rows(
        jnp.concatenate([rim_rows, mr_proj], axis=0).astype(jnp.float32), mr_short, row_count
    )
    queries = mr_mixed[:, 0]
    own_values = (mr_mixed[:, 1] * mr_mixed[:, 2]).astype(jnp.bfloat16)
    tail_rows = passed_along(own_values[-(tap_count - 1) :], "seq", 1)
    block_count = row_count // tap_count
    padded = jnp.concatenate(
        [tail_rows, own_values, jnp.zeros((1, chan_width), jnp.bfloat16)], axis=0
    )
    columns_major = padded.T.reshape(filter_count, GROUP, block_count + 1, tap_count)
    band_matrix = band_matrices(mr_filter)
    filtered_mr = jnp.einsum(
        "gis,gcbs->gcbi",
        band_matrix[:, :, :tap_count],
        columns_major[:, :, :-1],
        preferred_element_type=jnp.float32,
    )
    filtered_mr = filtered_mr + jnp.einsum(
        "gis,gcbs->gcbi",
        band_matrix[:, :, tap_count:],
        columns_major[:, :, 1:],
        preferred_element_type=jnp.float32,
    )
    filtered_rows = filtered_mr.reshape(chan_width, row_count).T
    gated = (queries * filtered_rows).astype(jnp.bfloat16)
    branch = branch_product(gated, out_weights)
    branch, pieces = lax.optimization_barrier((branch, pieces))
    in_own = assembled(pieces, "seq").reshape(width, 3 * own_count)
    summed = summed_rows(branch.reshape(chan_size, part, width), "chan")
    own_stream = lax.dynamic_slice_in_dim(stream_in, me * part, part, 0)
    stream = (own_stream.astype(jnp.float32) + summed).astype(jnp.bfloat16)
    stream_wide = stream.astype(jnp.float32)
    inverse_rms = lax.rsqrt(jnp.mean(stream_wide * stream_wide, axis=1, keepdims=True) + EPSILON)
    normed = (stream_wide * inverse_rms * li_gain[None]).astype(jnp.bfloat16)
    stream_parts = jnp.moveaxis(stream.reshape(part, chan_size, chan_width), 1, 0)
    if chan_size == 2:
        swap = [(0, 1), (1, 0)]
        stream_mine = lax.dynamic_index_in_dim(stream_parts, me, 0, keepdims=False)
        stream_other = lax.dynamic_index_in_dim(stream_parts, 1 - me, 0, keepdims=False)
        gathered, in_other, stream_other = gathered_rows(
            0, normed, in_own, stream_other
        )
        gathered = gathered.reshape(seq_size * part, width)
        stream_out = jnp.concatenate(
            [
                jnp.where(me == 0, stream_mine, stream_other),
                jnp.where(me == 0, stream_other, stream_mine),
            ]
        )

        def product(rows, matrix, low, high):
            return jnp.dot(
                rows,
                matrix[:, low * own_count : high * own_count],
                preferred_element_type=jnp.float32,
            ).astype(jnp.bfloat16)

        outgoing = product(gathered, in_other, 1, 3)
        sent = lax.ppermute(outgoing, "chan", swap)
        later, _ = lax.optimization_barrier((gathered, outgoing))
        outgoing_opener = product(later, in_other, 0, 1)
        sent_opener = lax.ppermute(outgoing_opener, "chan", swap)
        last, _ = lax.optimization_barrier((gathered, outgoing_opener))
        kept = product(last, in_own, 0, 3)
        kept, li_rate = lax.optimization_barrier((kept, li_rate))
        received = (sent_opener, sent[:, :own_count], sent[:, own_count:])

        def ordered(index):
            mine = kept[:, index * own_count : (index + 1) * own_count].T
            theirs = received[index].T
            pair = [
                jnp.where(me == 0, mine, theirs).reshape(own_count, seq_size, 1, part),
                jnp.where(me == 0, theirs, mine).reshape(own_count, seq_size, 1, part),
            ]
            return jnp.concatenate(pair, axis=2).reshape(own_count, seq_size * row_count)
    else:
        stream_out = swapped(stream_parts, "chan").reshape(row_count, chan_width)
        gathered = gathered_rows(0, normed)[0].reshape(seq_size * part, width)
        in_all = lax.all_gather(in_own, "chan", axis=0)
        raw = jnp.einsum(
            "xdn,td->xnt", in_all, gathered, preferred_element_type=jnp.float32
        ).astype(jnp.bfloat16)
        raw = swapped(raw, "chan").reshape(chan_size, 3, own_count, seq_size, part)
        raw = jnp.transpose(raw, (1, 2, 3, 0, 4)).reshape(3, own_count, seq_size * row_count)

        def ordered(index):
            return raw[index]

    keys, gates = ordered(1), ordered(2)
    seq_offset = lax.axis_index("seq") * own_count
    own_short = lax.dynamic_slice_in_dim(li_short, seq_offset, own_count, 2)
    own_res = lax.dynamic_slice_in_dim(li_res, seq_offset, own_count, 1)
    own_rate = lax.dynamic_slice_in_dim(li_rate, seq_offset, own_count, 1)
    own_skip = lax.dynamic_slice_in_dim(li_skip, seq_offset, own_count, 0)
    values = (lagged_time(keys, own_short[1]) * lagged_time(gates, own_short[2])).astype(
        jnp.bfloat16
    )
    filtered = modal_filter(values, own_res, own_rate, own_skip)
    if chan_size == 2:
        filtered, sent_opener = lax.optimization_barrier((filtered, sent_opener))
        received = (sent_opener,) + received[1:]
    openers = ordered(0)
    result = (lagged_time(openers, own_short[0]) * filtered).astype(jnp.bfloat16)
    li_output = lax.all_to_all(result, "seq", split_axis=1, concat_axis=0, tiled=True)
    return (stream_out, li_output)


HALVES = 2
PLANE = 8
SIB, NEAR, FAR, ACROSS = 1, 2, 4, 8
LANES = 128
RIM = 16


def flipped(bit, flip):
    return bit + flip - 2 * bit * flip


class Place:
    def __init__(self):
        self.seat = lax.axis_index("seq")
        self.side = lax.axis_index("chan")
        self.half = self.seat // PLANE
        self.spot = lax.rem(self.seat, PLANE)
        self.bits = (lax.rem(self.spot, 2), lax.rem(self.spot // 2, 2), self.spot // 4)

    def spot_at(self, code):
        return sum(flipped(self.bits[i], (code >> i) & 1) << i for i in range(3))

    def pair_at(self, code):
        return flipped(self.bits[1], code & 1) + 2 * flipped(self.bits[2], (code >> 1) & 1)

    def half_at(self, flip):
        return flipped(self.half, flip)

    def side_at(self, code):
        return flipped(self.side, (code >> 3) & 1)

    def target(self, flip, code):
        if code == ACROSS:
            return {"chan": 1 - self.side}
        return {"seq": self.half_at(flip) * PLANE + self.spot_at(code)}


def tapped(extended, weights, start, rows):
    total = weights[0:1] * extended[start : start + rows]
    for lag in (1, 2):
        total = total + weights[lag : lag + 1] * extended[start - lag : start - lag + rows]
    return total


def added(terms):
    while len(terms) > 1:
        odd = terms[-1:] if len(terms) % 2 else []
        terms = [a + b for a, b in zip(terms[::2], terms[1::2])] + odd
    return terms[0]


def window(start, size):
    return pl.ds(pl.multiple_of(start, size), size)


TURNED = ()
SAME = (0, 1, 4, 5)
CROSS = (2, 3, 6, 7)


def pieces_of(flip, group, codes):
    return [(flip, code, group) for code in codes if (flip, code) != (0, 0)]


INNER_FIRST = []
INNER_REST = (
    pieces_of(1, 0, SAME + CROSS) + pieces_of(0, 0, SAME + CROSS) + pieces_of(1, 1, SAME + CROSS)
    + pieces_of(0, 1, SAME + CROSS)
)
OUTER_FIRST = []
OUTER_REST = (
    pieces_of(1, 0, SAME + CROSS) + pieces_of(0, 0, SAME + CROSS) + pieces_of(1, 1, SAME + CROSS)
    + pieces_of(0, 1, SAME + CROSS)
)
PACE = 1


def layer_kernel(
    proj_in, stream_in, out_weights, weights, mr_short_in, filter_in, gain_in, li_short_in, res_in,
    rate_in, skip_in, stream_ref, out_ref,
    proj, extended_values, rim, mr_short, filters, gain, base, li_short, res, rate, skip,
    gated, cols, kept, outgoing, incoming, base_rows, block, spread, pieces,
    lent, inverse, mixed, edge, values, partial, ends, starts, state_out, state_in, turned,
    load_sem, halo_send, halo_recv, w_sem, sin_send, sin_recv, gat_send, gat_recv, x_send, x_recv,
    a_send, a_recv, b_send, b_recv, edge_sem, state_sem, out_send, out_recv,
):
    place = Place()
    spot, half, side, seat = place.spot, place.half, place.side, place.seat
    seats = lax.axis_size("seq")
    _, rows, depth = proj.shape
    part = rows // 2
    wide = cols.shape[2]
    taps = filters.shape[1]
    chans = pieces.shape[4]
    groups = chans // LANES
    modes = res.shape[0]
    everyone = [(f, r) for f in (0, 1) for r in range(PLANE) if (f, r) != (0, 0)]
    started = []
    counter = iter(range(load_sem.shape[0]))

    def load(source, target):
        copy = pltpu.make_async_copy(source, target, load_sem.at[next(counter)])
        copy.start()
        return copy

    first_loads = [
        load(proj_in, proj), load(mr_short_in, mr_short), load(filter_in, filters),
    ]
    gain_loads = [
        load(weights, lent), load(gain_in, gain),
    ]
    mine = window(side * part, part)
    late_loads = [
        load(out_weights, cols.at[0]), load(li_short_in, li_short), load(res_in, res),
        load(rate_in, rate), load(skip_in, skip),
    ]
    for f in (0, 1):
        at = window((place.half_at(f) * PLANE + spot) * wide, wide)
        late_loads.append(
            load(stream_in.at[mine, at], base_rows.at[spot, :, pl.ds(f * wide, wide)])
        )

    barrier = pltpu.get_barrier_semaphore()
    for f, r in everyone:
        pl.semaphore_signal(barrier, inc=1, device_id=place.target(f, r))
    pl.semaphore_signal(barrier, inc=1, device_id=place.target(0, ACROSS))
    pl.semaphore_wait(barrier, len(everyone) + 1)

    def remote(source, lands, send, recv, target):
        return pltpu.make_async_remote_copy(
            src_ref=source, dst_ref=lands, send_sem=send, recv_sem=recv, device_id=target
        )

    def go(copy):
        copy.start()
        started.append(copy)

    following = {"seq": jnp.minimum(seat + 1, seats - 1)}
    halo = [
        remote(
            proj_in.at[:, pl.ds(rows - RIM, RIM)], rim,
            halo_send.at[0], halo_recv.at[0], following,
        ),
        remote(
            extended_values.at[pl.ds(rows, taps)], extended_values.at[pl.ds(0, taps)],
            halo_send.at[1], halo_recv.at[1], following,
        ),
    ]

    @pl.when(seat < seats - 1)
    def _():
        halo[0].start()

    for copy in first_loads:
        copy.wait()
    tiles = depth // LANES

    def keep_values(parts, first, count, at):
        extended_values[pl.ds(taps + first, count), at] = (parts[0] * parts[1]).astype(jnp.bfloat16)

    def inner_values(i, carry):
        at = window(i * LANES, LANES)
        parts = [
            tapped(
                proj[p, taps - RIM : rows, at].astype(jnp.float32), mr_short[p, :, at], RIM, rows - taps
            )
            for p in (1, 2)
        ]
        keep_values(parts, taps, rows - taps, at)
        return carry

    def outer_values(i, carry):
        at = window(i * LANES, LANES)
        parts = [
            tapped(
                jnp.concatenate([rim[p, :, at], proj[p, 0:taps, at]], axis=0).astype(jnp.float32),
                mr_short[p, :, at], RIM, taps,
            )
            for p in (1, 2)
        ]
        keep_values(parts, 0, taps, at)
        return carry

    lax.fori_loop(0, tiles, inner_values, 0)

    @pl.when(seat < seats - 1)
    def _():
        halo[1].start()

    go(remote(out_weights, cols.at[1], w_sem.at[0], w_sem.at[1], place.target(1, 0)))
    for code in range(1, PLANE):
        for f in (0, 1):
            at = window((place.half_at(f) * PLANE + place.spot_at(code)) * wide, wide)
            go(
                remote(
                    stream_in.at[mine, at], base_rows.at[spot, :, pl.ds(f * wide, wide)],
                    sin_send.at[code * 2 + f], sin_recv.at[code * 2 + f], place.target(0, code),
                )
            )

    def base_wait(code, f):
        lands = base_rows.at[place.spot_at(code), :, pl.ds(f * wide, wide)]
        remote(
            lands, lands, sin_send.at[0], sin_recv.at[code * 2 + f], place.target(0, SIB)
        ).wait_recv()

    subset = (pl.ds(1, 2), pl.ds(0, 1))

    def piece_copy(f, code, g):
        at = window(place.spot_at(code) * chans, chans)
        index = (g * 2 + f) * PLANE + code
        return remote(
            lent.at[subset[g], :, at], pieces.at[f, spot, subset[g]], b_send.at[index],
            b_recv.at[index], place.target(f, code),
        )

    def piece_wait(f, code, g):
        lands = pieces.at[f, place.spot_at(code), subset[g]]
        index = (g * 2 + f) * PLANE + code
        remote(lands, lands, b_send.at[0], b_recv.at[index], place.target(0, SIB)).wait_recv()

    inner = flipped(half, place.bits[2])

    def issue(inner_pieces, outer_pieces):
        for wanted, some in ((1, inner_pieces), (0, outer_pieces)):
            if some:

                @pl.when(inner == wanted)
                def _():
                    for piece in some:
                        piece_copy(*piece).start()

    queues = [list(INNER_REST), list(OUTER_REST)]

    def drip(count=PACE):
        taken = [queue[:count] for queue in queues]
        for queue in queues:
            del queue[:count]
        issue(*taken)

    source = lax.broadcasted_iota(jnp.int32, (taps, 2 * taps), 0)
    landing = lax.broadcasted_iota(jnp.int32, (taps, 2 * taps), 1)
    mirror = (source + landing == taps).astype(jnp.bfloat16)
    base[...] = jnp.dot(
        filters[...].astype(jnp.bfloat16), mirror, preferred_element_type=jnp.float32
    )

    @pl.when(seat > 0)
    def _():
        halo[0].wait_recv()

    @pl.when(seat == 0)
    def _():
        rim[...] = jnp.zeros_like(rim)
        extended_values[0:taps, :] = jnp.zeros((taps, depth), extended_values.dtype)

    lax.fori_loop(0, tiles, outer_values, 0)

    @pl.when(seat > 0)
    def _():
        halo[1].wait_recv()

    blocks = rows // taps
    lane = lax.broadcasted_iota(jnp.int32, (taps, blocks * LANES), 1)
    member = lax.rem(lane, LANES) // GROUP
    members = LANES // GROUP

    def mix(i, carry):
        at = window(i * LANES, LANES)
        operand = jnp.concatenate(
            [extended_values[b * taps : b * taps + 2 * taps, at] for b in range(blocks)], axis=1
        )
        table = base[window(i * members, members), :]
        picked = None
        for g in range(members):
            row = jnp.broadcast_to(table[g : g + 1, :], (taps, 2 * taps))
            band = pltpu.roll(row, 0, 1, stride=1, stride_axis=0).astype(jnp.bfloat16)
            product = jnp.dot(band, operand, preferred_element_type=jnp.float32)
            picked = product if picked is None else jnp.where(member == g, product, picked)
        extended = jnp.concatenate([rim[0, :, at], proj[0, :, at]], axis=0).astype(jnp.float32)
        queries = tapped(extended, mr_short[0, :, at], RIM, rows)
        for b in range(blocks):
            gated[spot, pl.ds(b * taps, taps), at] = (
                queries[b * taps : (b + 1) * taps] * picked[:, b * LANES : (b + 1) * LANES]
            ).astype(gated.dtype)
        return carry

    span = depth // 2

    def gather(dim, code, s):
        lands = gated.at[place.spot_at(code), :, pl.ds(s * span, span)]
        index = {SIB: 0, NEAR: 1, FAR: 2}[dim]
        go(
            remote(
                lands, lands, gat_send.at[(index * PLANE + code) * 2 + s],
                gat_recv.at[(code ^ dim) * 2 + s], place.target(0, dim),
            )
        )

    def gathered(code, s):
        lands = gated.at[place.spot_at(code), :, pl.ds(s * span, span)]
        remote(
            lands, lands, gat_send.at[0], gat_recv.at[code * 2 + s], place.target(0, SIB)
        ).wait_recv()

    lax.fori_loop(0, tiles // 2, mix, 0)
    for dim in (NEAR, FAR, SIB):
        gather(dim, 0, 0)
    lax.fori_loop(tiles // 2, tiles, mix, 0)
    for dim in (FAR, NEAR, SIB):
        gather(dim, 0, 1)

    for copy in gain_loads:
        copy.wait()
    deep = lent.shape[1]
    row = jnp.broadcast_to(gain[:, window(seat * deep, deep)], (PLANE, deep))
    column = jnp.broadcast_to(row.T[:, 0:1], (deep, LANES))

    def lend(i, carry):
        at = window(i * LANES, LANES)
        for p in range(3):
            lent[p, :, at] = (lent[p, :, at].astype(jnp.float32) * column).astype(lent.dtype)
        return carry

    lax.fori_loop(0, depth // LANES, lend, 0)
    late_loads.append(load(lent.at[:, :, window(spot * chans, chans)], pieces.at[0, spot]))
    issue(INNER_FIRST, OUTER_FIRST)

    def pair(code):
        return pl.ds(place.pair_at(code) * 2, 2)

    def swap(k, f):
        return remote(
            outgoing.at[k, f], incoming.at[k, f], x_send.at[k * 2 + f], x_recv.at[k * 2 + f],
            place.target(0, ACROSS),
        )

    def multiply(k, f):
        for who in (1, 0):
            at = window(flipped(side, who) * part, part)
            left = gated[pair(k), at, :].reshape(2 * part, depth)
            product = jnp.dot(left, cols[f], preferred_element_type=jnp.float32)
            product = product.reshape(2, part, wide)
            if who:
                outgoing[k, f] = product.astype(outgoing.dtype)
                go(swap(k, f))
            else:
                kept[k, f] = product

    a_counter = iter(range(a_send.shape[0]))
    a_started = []

    def spread_slot(code, k, f):
        return spread.at[
            f, place.spot_at(code & 7), pair(((code >> 1) & 3) ^ k), place.side_at(code)
        ]

    def scatter(dim, code, k, f):
        lands = spread_slot(code, k, f)
        copy = remote(
            block.at[k, f] if code == 0 else lands, lands,
            a_send.at[next(a_counter)], a_recv.at[((code ^ dim) * 4 + k) * 2 + f],
            place.target(0, dim),
        )
        copy.start()
        a_started.append(copy)

    def finish(k, f):
        swap(k, f).wait_recv()
        for code in (2 * k, 2 * k + 1):
            if code:
                base_wait(code, f)
        total = (
            base_rows[pair(k), :, f * wide : (f + 1) * wide].astype(jnp.float32)
            + kept[k, f]
            + incoming[k, f].astype(jnp.float32)
        )
        block[k, f] = total.astype(block.dtype)
        spread[f, spot, pair(k), side] = block[k, f]
        for dim in (ACROSS, FAR, NEAR, SIB):
            scatter(dim, 0, k, f)

    def onward(code, k, f):
        lands = spread_slot(code, k, f)
        remote(
            lands, lands, a_send.at[0], a_recv.at[(code * 4 + k) * 2 + f], place.target(0, SIB)
        ).wait_recv()
        if code & SIB:
            return
        order = (FAR, NEAR, ACROSS) if (k, f) not in TURNED else (FAR, ACROSS, NEAR)
        last = max(i for i, dim in enumerate(order) if code & dim)
        for dim in order[last + 1 :] + (SIB,):
            scatter(dim, code, k, f)
        if last < 2:
            drip()

    def both(action, *codes):
        for s in (0, 1):
            for code in codes:
                action(code, s)

    for copy in late_loads:
        copy.wait()
    both(gathered, SIB)
    multiply(0, 0)
    gathered(NEAR, 0)
    gather(FAR, NEAR, 0)
    gather(SIB, NEAR, 0)
    gathered(FAR, 1)
    gather(NEAR, FAR, 1)
    gather(SIB, FAR, 1)
    drip()
    finish(0, 0)
    gathered(NEAR, 1)
    gather(SIB, NEAR, 1)
    gathered(FAR, 0)
    gather(SIB, FAR, 0)
    drip()
    both(gathered, NEAR | SIB)
    drip()
    multiply(1, 0)
    both(gathered, FAR | SIB)
    drip()
    multiply(2, 0)
    finish(1, 0)
    onward(FAR, 0, 0)
    for s in (0, 1):
        gathered(NEAR | FAR, s)
        gather(SIB, NEAR | FAR, s)
    finish(2, 0)
    drip()
    both(gathered, NEAR | FAR | SIB)
    drip()
    multiply(3, 0)
    onward(NEAR, 0, 0)
    onward(FAR, 1, 0)
    onward(FAR, 2, 0)
    onward(NEAR | FAR, 0, 0)
    finish(3, 0)
    drip()
    remote(cols.at[1], cols.at[1], w_sem.at[0], w_sem.at[1], place.target(1, 0)).wait_recv()
    multiply(0, 1)
    multiply(1, 1)
    finish(0, 1)
    multiply(2, 1)
    finish(1, 1)
    multiply(3, 1)
    finish(2, 1)
    finish(3, 1)
    drip()
    onward(NEAR, 1, 0)
    onward(NEAR, 2, 0)
    for f in (0, 1):
        for k in range(4):
            for code in (FAR, NEAR, ACROSS, NEAR | FAR, ACROSS | FAR):
                done = (FAR, 0, 0), (NEAR, 0, 0), (FAR, 1, 0), (FAR, 2, 0), (NEAR | FAR, 0, 0)
                done += (NEAR, 1, 0), (NEAR, 2, 0)
                pivot = ACROSS if (k, f) in TURNED else NEAR
                if (code, k, f) not in done and (code == FAR or code & pivot):
                    onward(code, k, f)
    drip(2 * len(INNER_REST))
    for f in (0, 1):
        for k in range(4):
            pivot = NEAR if (k, f) in TURNED else ACROSS
            for code in range(2, 16, 2):
                if code & pivot:
                    onward(code, k, f)
    for f in (0, 1):
        for k in range(4):
            for code in range(1, 16, 2):
                onward(code, k, f)

    stream_copies = []
    for other in range(PLANE):
        stream_copies.append(
            load(
                spread.at[flipped(half, side), other, spot],
                stream_ref.at[:, :, pl.ds(other * wide, wide)],
            )
        )

    width = PLANE * HALVES * wide

    couples = PLANE // 2
    double = 2 * rows

    def product(couple, g):
        left = [
            spread[f, other, pl.ds(2 * couple, 2)].reshape(double, wide)
            for f in range(HALVES)
            for other in range(PLANE)
        ]
        where = window(couple * double, double)
        if g == 0:
            squares = None
            for piece in left:
                piece = piece.astype(jnp.float32)
                for at in range(0, wide, LANES):
                    term = piece[:, at : at + LANES] * piece[:, at : at + LANES]
                    squares = term if squares is None else squares + term
            mean = jnp.sum(squares, axis=1, keepdims=True) / width
            inverse[where, :] = jnp.broadcast_to(lax.rsqrt(mean + EPSILON), (double, LANES))
        scale = inverse[where, :]
        left = jnp.concatenate(left, axis=1)
        at = pl.ds(pl.multiple_of(RIM + couple * double, RIM), double)
        for slot, p in enumerate((1, 2) if g == 0 else (0,)):
            right = pieces[:, :, p].reshape(width, chans)
            raw = jnp.dot(left, right, preferred_element_type=jnp.float32)
            for c in range(groups):
                lanes = slice(c * LANES, (c + 1) * LANES)
                mixed[slot, at, lanes] = (
                    (raw[:, lanes] * scale).astype(jnp.bfloat16).astype(jnp.float32)
                )

    later = (half > 0).astype(jnp.float32)
    other_half = place.target(1, 0)
    my_chans = window(spot * chans, chans)

    def projected(g):
        for f, code in everyone:
            piece_wait(f, code, g)
        count = 2 - g
        lax.fori_loop(couples - 1, couples, lambda i, c: (product(i, g), c)[1], 0)
        rim_copy = remote(
            mixed.at[pl.ds(0, count), pl.ds(PLANE * rows, RIM)], edge.at[pl.ds(2 * g, count)],
            edge_sem.at[g * 2], edge_sem.at[g * 2 + 1], other_half,
        )
        rim_copy.start()
        lax.fori_loop(0, couples - 1, lambda i, c: (product(i, g), c)[1], 0)
        rim_copy.wait()
        mixed[0:count, 0:RIM, :] = edge[2 * g : 2 * g + count] * later

    def short_filtered(slot_index, p, slot):
        weights_of = li_short[p, :, my_chans]
        start = RIM + slot * rows
        total = weights_of[0:1] * mixed[slot_index, start : start + rows, :]
        for lag in (1, 2):
            total = total + weights_of[lag : lag + 1] * mixed[
                slot_index, start - lag : start - lag + rows, :
            ]
        return total

    def lane_group(c):
        return slice(c * LANES, (c + 1) * LANES)

    projected(0)
    for slot in range(PLANE):
        value = short_filtered(0, 1, slot) * short_filtered(1, 2, slot)
        value = value.astype(jnp.bfloat16).astype(jnp.float32)
        for c in range(groups):
            values[c, slot * rows : (slot + 1) * rows, :] = value[:, lane_group(c)]

    def spreaded(table, r):
        return jnp.broadcast_to(table[r : r + 1], (PLANE, LANES))

    rates = rate[:, my_chans]
    gains = res[:, my_chans]
    decay = jnp.exp(-rates)
    leap = jnp.exp(-rates * rows)
    for c in range(groups):
        decays = [spreaded(decay[:, lane_group(c)], r) for r in range(modes)]
        weighted = [spreaded(gains[:, lane_group(c)], r) for r in range(modes)]

        def step(t, states):
            where = pl.ds(t, PLANE, stride=rows)
            value = values[c, where, :]
            states = tuple(d * s + value for d, s in zip(decays, states))
            partial[c, where, :] = added([w * s for w, s in zip(weighted, states)])
            return states

        states = lax.fori_loop(
            0, rows, step, tuple(jnp.zeros((PLANE, LANES), jnp.float32) for _ in range(modes)),
            unroll=4,
        )
        for r in range(modes):
            ends[:, r, lane_group(c)] = states[r]
    total = jnp.zeros((modes, chans), jnp.float32)
    for slot in range(PLANE):
        total = leap * total + ends[slot]
    state_out[...] = total
    state_copy = remote(state_out, state_in, state_sem.at[0], state_sem.at[1], other_half)
    state_copy.start()
    state_copy.wait()
    total = state_in[...] * later
    opening = gains * decay
    for slot in range(PLANE):
        first = opening * total
        for r in range(modes):
            starts[r, slot : slot + 1, :] = first[r : r + 1]
        total = leap * total + ends[slot]
    for c in range(groups):
        decays = [spreaded(decay[:, lane_group(c)], r) for r in range(modes)]
        direct = spreaded(skip[:, my_chans][:, lane_group(c)], 0)

        def close(t, states):
            where = pl.ds(t, PLANE, stride=rows)
            partial[c, where, :] = added(
                list(states) + [partial[c, where, :], direct * values[c, where, :]]
            )
            return tuple(d * s for d, s in zip(decays, states))

        lax.fori_loop(
            0, rows, close, tuple(starts[r, :, lane_group(c)] for r in range(modes)), unroll=4
        )

    projected(1)
    for slot in range(PLANE):
        opener = short_filtered(0, 0, slot)
        for c in range(groups):
            gated_rows = opener[:, lane_group(c)] * partial[c, slot * rows : (slot + 1) * rows, :]
            turned[slot, c * LANES : (c + 1) * LANES, :] = gated_rows.T.astype(turned.dtype)
    for code in range(1, PLANE):
        go(
            remote(
                turned.at[place.spot_at(code)], out_ref.at[my_chans], out_send.at[code],
                out_recv.at[code], place.target(0, code),
            )
        )
    stream_copies.append(load(turned.at[spot], out_ref.at[my_chans]))
    for code in range(1, PLANE):
        lands = out_ref.at[window(place.spot_at(code) * chans, chans)]
        remote(
            turned.at[0], lands, out_send.at[0], out_recv.at[code], place.target(0, SIB)
        ).wait_recv()
    for copy in stream_copies:
        copy.wait()
    for copy in started + a_started:
        copy.wait_send()
    for g in (0, 1):
        for f, code in everyone:
            piece_copy(f, code, g).wait_send()

    @pl.when(seat < seats - 1)
    def _():
        for copy in halo:
            copy.wait_send()


def layer(proj, stream_in, out_weights, weights, mr_short, filters, gain, li_short, res, rate, skip):
    _, rows, width = proj.shape
    part = rows // 2
    depth, wide = out_weights.shape
    deep = weights.shape[1]
    chans = width // PLANE
    groups = chans // LANES
    taps = filters.shape[1]
    modes = res.shape[0]
    length = PLANE * rows
    dma = pltpu.SemaphoreType.DMA
    anywhere = pl.BlockSpec(memory_space=pl.ANY)
    bf16, f32 = jnp.bfloat16, jnp.float32
    vmem = pltpu.VMEM
    return pl.pallas_call(
        layer_kernel,
        out_shape=[
            jax.ShapeDtypeStruct((2, part, PLANE * wide), bf16),
            jax.ShapeDtypeStruct((width, rows), bf16),
        ],
        in_specs=[anywhere] * 11,
        out_specs=[anywhere] * 2,
        scratch_shapes=[
            vmem(proj.shape, bf16),
            vmem((taps + rows, width), bf16),
            vmem((3, RIM, width), bf16),
            vmem(mr_short.shape, f32),
            vmem(filters.shape, f32),
            vmem(gain.shape, f32),
            vmem((filters.shape[0], 2 * taps), f32),
            vmem(li_short.shape, f32),
            vmem(res.shape, f32),
            vmem(rate.shape, f32),
            vmem(skip.shape, f32),
            vmem((PLANE, rows, depth), bf16),
            vmem((HALVES, depth, wide), bf16),
            vmem((4, HALVES, 2, part, wide), f32),
            vmem((4, HALVES, 2, part, wide), bf16),
            vmem((4, HALVES, 2, part, wide), bf16),
            vmem((PLANE, part, HALVES * wide), bf16),
            vmem((4, HALVES, 2, part, wide), bf16),
            vmem((HALVES, PLANE, PLANE, 2, part, wide), bf16),
            vmem((HALVES, PLANE, 3, deep, chans), bf16),
            vmem(weights.shape, bf16),
            vmem((length, LANES), f32),
            vmem((2, RIM + length, chans), f32),
            vmem((3, RIM, chans), f32),
            vmem((groups, length, LANES), f32),
            vmem((groups, length, LANES), f32),
            vmem((PLANE, modes, chans), f32),
            vmem((modes, PLANE, chans), f32),
            vmem((modes, chans), f32),
            vmem((modes, chans), f32),
            vmem((PLANE, chans, rows), bf16),
            dma((32,)),
            dma((2,)),
            dma((2,)),
            dma((2,)),
            dma((2 * PLANE,)),
            dma((2 * PLANE,)),
            dma((3 * PLANE * 2,)),
            dma((PLANE * 2,)),
            dma((8,)),
            dma((8,)),
            dma((15 * 4 * HALVES,)),
            dma((16 * 4 * HALVES,)),
            dma((4 * PLANE,)),
            dma((4 * PLANE,)),
            dma((4,)),
            dma((2,)),
            dma((PLANE,)),
            dma((PLANE,)),
        ],
        compiler_params=pltpu.CompilerParams(
            collective_id=2, has_side_effects=True, vmem_limit_bytes=63 * 1024 * 1024
        ),
    )(proj, stream_in, out_weights, weights, mr_short, filters, gain, li_short, res, rate, skip)


def local_halves(
    stream_in,
    mr_proj,
    mr_short,
    mr_filter,
    mr_out,
    li_gain,
    li_in,
    li_short,
    li_res,
    li_rate,
    li_skip,
):
    row_count, _, width = mr_proj.shape
    stream, filtered = layer(
        jnp.transpose(mr_proj, (1, 0, 2)), stream_in, mr_out, jnp.transpose(li_in, (1, 0, 2)),
        mr_short, mr_filter, li_gain[None], li_short, li_res, li_rate, li_skip[None],
    )
    return stream.reshape(row_count, width), filtered


def local(*arrays):
    halves = lax.axis_size("chan") == 2 and lax.axis_size("seq") == HALVES * PLANE
    halves = halves and arrays[1].shape[0] >= 2 * arrays[3].shape[1]
    return (local_halves if halves else local_general)(*arrays)


def solution(mesh):
    in_specs = (
        P("seq", None),
        P("seq", None, "chan"),
        P(None, None, "chan"),
        P("chan", None),
        P("chan", "seq"),
        P(),
        P("seq", None, "chan"),
        P(None, None, "chan"),
        P(None, "chan"),
        P(None, "chan"),
        P("chan"),
    )
    out_specs = (P("seq", "chan"), P("chan", "seq"))
    return jax.shard_map(local, mesh=mesh, in_specs=in_specs, out_specs=out_specs, check_vma=False)
```
